32 devices in a mesh: dp: 4 (over x, core), seq: 8 (over z, y).
Axes of the slice: x: 2, y: 2, z: 4, core: 2. Of those that a mesh axis runs over, the one named last changes fastest.
Arguments:
- xbc_in: bfloat16 [4, 2048, 2816], P('dp', 'seq'), may hold values from -4 to 4
- conv_weight: float32 [4, 2816], replicated, may hold values from -3 to 3
- conv_bias: float32 [2816], replicated, may hold values from -3 to 3
- step_sizes: float32 [4, 40, 2048], P('dp', None, 'seq'), may hold values from 0 to 1, as said below
- decay_rates: float32 [40], replicated, may hold values from 0.7 to 1.4
- skip_gain: float32 [40], replicated, may hold values from 0.5 to 1.5
- grad_out: bfloat16 [4, 2048, 2560], P('dp', 'seq'), may hold values from -0.75 to 0.75
Outputs:
- grad_xbc: bfloat16 [4, 2048, 2816], P('dp', 'seq')
- grad_steps: float32 [4, 40, 2048], P('dp', None, 'seq')
- grad_conv_weight: float32 [4, 2816], replicated
- grad_conv_bias: float32 [2816], replicated
- grad_rates: float32 [40], replicated
- grad_skip: float32 [40], replicated
The draws below stay inside these ranges and needn't reach their ends.
Inputs may be any that keep to these rules, and one draw needn't show every extreme that they name: `step_sizes`: positive step sizes.
All inputs are finite; a program needn't handle non-finite values.
Results may differ from the reference program's by a relative error of at most 0.0056.
Values may be sent and summed in bfloat16 or wider, within the bound.
A program may use at most 192 MiB of HBM per device.

```python
import math
import jax
import jax.numpy as jnp
from jax import lax

HEADS = 40
HEAD_DIM = 64
STATE = 128
GROUP = 256
KCONV = 4
TOKENS_PER_SEQ = 2048
BATCH_SEQUENCES = 4
CH = 2816


def draw_step_sizes(key, part):
    random_split_keys = jax.random.split(jax.random.fold_in(key, 11), 5)
    fast_count = 5
    slow_log = jax.random.uniform(random_split_keys[0], (BATCH_SEQUENCES, HEADS, 1), jnp.float32, math.log(0.8), math.log(3.3))
    slow_rate = jnp.exp(slow_log) / TOKENS_PER_SEQ
    fast_head = jax.random.randint(random_split_keys[1], (BATCH_SEQUENCES, HEADS, 1), 0, 20) < fast_count
    baseline_rate = jnp.where(fast_head, 1.0 / 40.0, slow_rate)
    jaggedness = jax.random.uniform(random_split_keys[2], (BATCH_SEQUENCES, HEADS, TOKENS_PER_SEQ), jnp.float32, 0.5, 1.5)
    spike_position = jax.random.randint(random_split_keys[3], (BATCH_SEQUENCES, 1, 1, 4), 0, TOKENS_PER_SEQ)
    token_position = lax.broadcasted_iota(jnp.int32, (BATCH_SEQUENCES, 1, TOKENS_PER_SEQ, 4), 2)
    spike_mask = jnp.any(token_position == spike_position, axis=3)
    spike_length = jax.random.uniform(random_split_keys[4], (BATCH_SEQUENCES, 1, TOKENS_PER_SEQ), jnp.float32, 0.22, 0.7)
    return baseline_rate * jaggedness + jnp.where(spike_mask, spike_length, 0.0)


def levels(rng, dims, pieces, low, largest):
    gain, own = 1.0, jax.random.fold_in(rng, 6)
    for position, blocks in pieces:
        heights = jnp.exp(jax.random.uniform(jax.random.fold_in(own, position), (blocks,), jnp.float32, low / len(pieces), largest / len(pieces)))
        gain = gain * jnp.repeat(heights, dims[position] // blocks).reshape([-1 if axis == position else 1 for axis in range(len(dims))])
    return gain


def noise(stream_key, extent, spread, most, pieces=(), dtype=jnp.bfloat16):
    factor_of = levels(stream_key, extent, pieces, -0.22, 0.18) if pieces else 1.0
    values = jax.random.normal(stream_key, extent, jnp.float32) * spread * factor_of
    return jnp.minimum(jnp.maximum(values, -most), most).astype(dtype)


def setup_inputs(seed: int = 0) -> dict:
    seeds = jax.random.split(jax.random.key(seed), 8)
    return {
        "xbc_in": noise(seeds[0], (BATCH_SEQUENCES, TOKENS_PER_SEQ, CH), 0.3, 4.0, ((0, 4), (1, 8))),
        "conv_weight": noise(seeds[1], (KCONV, CH), KCONV ** -0.5, 3.0, (), jnp.float32),
        "conv_bias": noise(seeds[2], (CH,), 0.2, 3.0, (), jnp.float32),
        "step_sizes": draw_step_sizes(jax.random.fold_in(seeds[7], 71), 0),
        "decay_rates": jnp.clip(jnp.exp(jax.random.uniform(seeds[4], (HEADS,), jnp.float32, math.log(0.7), math.log(1.4))), 0.7, 1.4),
        "skip_gain": jnp.clip(jax.random.uniform(seeds[5], (HEADS,), jnp.float32, 0.5, 1.5), 0.5, 1.5),
        "grad_out": noise(seeds[6], (BATCH_SEQUENCES, TOKENS_PER_SEQ, HEADS * HEAD_DIM), 0.05, 0.75, ((0, 4), (1, 8))),
    }


def silu_pair(pre_act):
    sigmoid_v = jax.nn.sigmoid(pre_act)
    return pre_act * sigmoid_v, sigmoid_v * (1.0 + pre_act * (1.0 - sigmoid_v))


def split_block(z_block, dy_block, cum_log):
    x_width = HEADS * HEAD_DIM
    x_heads = z_block[:, :x_width].astype(jnp.float32).reshape(GROUP, HEADS, HEAD_DIM)
    b_proj = z_block[:, x_width:x_width + STATE]
    c_proj = z_block[:, x_width + STATE:]
    dy_heads = dy_block.astype(jnp.float32).reshape(GROUP, HEADS, HEAD_DIM)
    log_end = cum_log[:, -1:]
    tail_decay = jnp.exp(log_end - cum_log).T
    x_weighted = (x_heads * tail_decay[:, :, None]).astype(jnp.bfloat16)
    dy_weighted = (dy_heads * jnp.exp(cum_log).T[:, :, None]).astype(jnp.bfloat16)
    return x_heads, b_proj, c_proj, dy_heads, log_end, tail_decay, x_weighted, dy_weighted


def block_locals(z_block, dy_block, cum_log):
    x_heads, b_proj, c_proj, dy_heads, log_end, tail_decay, x_weighted, dy_weighted = split_block(z_block, dy_block, cum_log)
    s_local = jnp.einsum("sn,shp->hpn", b_proj.astype(jnp.float32), x_weighted.astype(jnp.float32))
    u_local = jnp.einsum("sn,shp->hpn", c_proj.astype(jnp.float32), dy_weighted.astype(jnp.float32))
    return s_local, u_local


def block_grads(z_block, dy_block, cum_log, start_state, end_adjoint, skip_gain):
    x_heads, b_proj, c_proj, dy_heads, log_end, tail_decay, x_weighted, dy_weighted = split_block(z_block, dy_block, cum_log)
    gram_bc = jnp.dot(b_proj, c_proj.T, preferred_element_type=jnp.float32)
    row_index = lax.broadcasted_iota(jnp.int32, (GROUP, GROUP), 0)
    col_index = lax.broadcasted_iota(jnp.int32, (GROUP, GROUP), 1)
    causal = (row_index >= col_index)[None]
    log_gap = cum_log[:, :, None] - cum_log[:, None, :]
    decay_lower = jnp.where(causal, jnp.exp(jnp.where(causal, log_gap, 0.0)), 0.0)
    inner_dx = jnp.einsum("thp,shp->hts", dy_heads, x_heads)
    weights = decay_lower * inner_dx
    k_matrix = (jnp.swapaxes(decay_lower, 1, 2) * gram_bc[None]).astype(jnp.bfloat16)
    m_terms = weights * gram_bc.T[None]
    w_summed = jnp.sum(weights, axis=0).astype(jnp.bfloat16)
    states_low = start_state.astype(jnp.bfloat16).astype(jnp.float32)
    adjoint_low = end_adjoint.astype(jnp.bfloat16).astype(jnp.float32)
    b_float = b_proj.astype(jnp.float32)
    c_float = c_proj.astype(jnp.float32)
    b_adjoint = jnp.einsum("tn,hpn->thp", b_float, adjoint_low)
    dx_state = jnp.einsum("hts,shp->thp", k_matrix.astype(jnp.float32), dy_heads) + tail_decay[:, :, None] * b_adjoint
    grad_bproj = jnp.dot(w_summed.T, c_proj, preferred_element_type=jnp.float32) + jnp.einsum("thp,hpn->tn", x_weighted.astype(jnp.float32), adjoint_low)
    grad_cproj = jnp.dot(w_summed, b_proj, preferred_element_type=jnp.float32) + jnp.einsum("thp,hpn->tn", dy_weighted.astype(jnp.float32), states_low)
    c_state = jnp.einsum("tn,hpn->thp", c_float, states_low)
    q_terms = jnp.sum(c_state * dy_heads, axis=2).T
    r_terms = jnp.sum(b_adjoint * x_heads, axis=2).T
    col_sums = jnp.sum(m_terms, axis=1)
    row_sums = jnp.sum(m_terms, axis=2)
    term_one = jnp.cumsum(col_sums - row_sums, axis=1) + row_sums
    term_two = jnp.flip(jnp.cumsum(jnp.flip(jnp.exp(cum_log) * q_terms, 1), axis=1), 1)
    term_three = jnp.cumsum(jnp.exp(log_end - cum_log) * r_terms, axis=1)
    term_four = jnp.exp(log_end) * jnp.sum(end_adjoint * start_state, axis=(1, 2))[:, None]
    grad_log = term_one + term_two + term_three + term_four - jnp.sum(x_heads * dx_state, axis=2).T
    dx_full = dx_state + skip_gain[None, :, None] * dy_heads
    grad_z = jnp.concatenate([dx_full.reshape(GROUP, HEADS * HEAD_DIM), grad_bproj, grad_cproj], axis=1)
    return grad_z, grad_log


def one_sequence(xbc_seq, step_seq, dy_seq, conv_weight, conv_bias, decay_rates, skip_gain):
    rim_len = KCONV - 1
    x_width = HEADS * HEAD_DIM
    padded_in = jnp.concatenate([jnp.zeros((rim_len, CH), jnp.bfloat16), xbc_seq], axis=0)
    pre_act = jnp.zeros((TOKENS_PER_SEQ, CH), jnp.float32) + conv_bias[None, :]
    for tap_index in range(KCONV):
        pre_act = pre_act + conv_weight[tap_index][None, :] * padded_in[tap_index:tap_index + TOKENS_PER_SEQ].astype(jnp.float32)
    activated, derivative = silu_pair(pre_act)
    z_seq = activated.astype(jnp.bfloat16)
    block_count = TOKENS_PER_SEQ // GROUP
    log_steps = -(step_seq * decay_rates[:, None])
    cum_log = jnp.transpose(jnp.cumsum(log_steps.reshape(HEADS, block_count, GROUP), axis=2), (1, 0, 2))
    z_blocks = z_seq.reshape(block_count, GROUP, CH)
    dy_blocks = dy_seq.reshape(block_count, GROUP, x_width)
    s_local, u_local = lax.map(lambda block_item: block_locals(block_item[0], block_item[1], block_item[2]), (z_blocks, dy_blocks, cum_log))
    decay_end = jnp.exp(cum_log[:, :, -1])

    def advance(carried, block_item):
        return block_item[0][:, None, None] * carried + block_item[1], carried

    zero_state = jnp.zeros((HEADS, HEAD_DIM, STATE), jnp.float32)
    unused_one, block_starts = lax.scan(advance, zero_state, (decay_end, s_local))
    unused_two, block_ends = lax.scan(advance, zero_state, (decay_end, u_local), reverse=True)
    grad_z, grad_log = lax.map(lambda block_item: block_grads(block_item[0], block_item[1], block_item[2], block_item[3], block_item[4], skip_gain), (z_blocks, dy_blocks, cum_log, block_starts, block_ends))
    grad_pre = grad_z.reshape(TOKENS_PER_SEQ, CH) * derivative
    grad_log = jnp.transpose(grad_log, (1, 0, 2)).reshape(HEADS, TOKENS_PER_SEQ)
    padded_grad = jnp.concatenate([grad_pre, jnp.zeros((rim_len, CH), jnp.float32)], axis=0)
    grad_in = jnp.zeros((TOKENS_PER_SEQ, CH), jnp.float32)
    grad_taps = []
    for tap_index in range(KCONV):
        tap_start = rim_len - tap_index
        grad_in = grad_in + conv_weight[tap_index][None, :] * padded_grad[tap_start:tap_start + TOKENS_PER_SEQ]
        grad_taps.append(jnp.sum(grad_pre * padded_in[tap_index:tap_index + TOKENS_PER_SEQ].astype(jnp.float32), axis=0))
    grad_weight = jnp.stack(grad_taps)
    grad_bias = jnp.sum(grad_pre, axis=0)
    grad_steps = -decay_rates[:, None] * grad_log
    grad_rates = -jnp.sum(step_seq * grad_log, axis=1)
    skip_terms = (z_seq[:, :x_width].astype(jnp.float32) * dy_seq.astype(jnp.float32)).reshape(TOKENS_PER_SEQ, HEADS, HEAD_DIM)
    grad_skip = jnp.sum(skip_terms, axis=(0, 2))
    return grad_in.astype(jnp.bfloat16), grad_steps, grad_weight, grad_bias, grad_rates, grad_skip


def reference(xbc_in, conv_weight, conv_bias, step_sizes, decay_rates, skip_gain, grad_out):
    results = lax.map(lambda seq_item: one_sequence(seq_item[0], seq_item[1], seq_item[2], conv_weight, conv_bias, decay_rates, skip_gain), (xbc_in, step_sizes, grad_out))
    grad_in, grad_steps, grad_weight, grad_bias, grad_rates, grad_skip = results
    return (grad_in, grad_steps, jnp.sum(grad_weight, axis=0), jnp.sum(grad_bias, axis=0), jnp.sum(grad_rates, axis=0), jnp.sum(grad_skip, axis=0))
```

```python
import functools
import jax
import jax.numpy as jnp
from jax import lax
from jax.experimental import pallas as pl
from jax.experimental.pallas import tpu as pltpu
from jax.sharding import PartitionSpec as P

HEADS = 40
HEAD_DIM = 64
STATE = 128
GROUP = 256
KCONV = 4
XW = HEADS * HEAD_DIM
CH = XW + 2 * STATE
TILE = 256
HALF = HEADS // 2
CHUNK = 5
NCHUNK = HALF // CHUNK
MESH = pl.DeviceIdType.MESH
F32 = jnp.float32
BF16 = jnp.bfloat16
HI = lax.Precision.HIGHEST
VM = functools.partial(pl.BlockSpec, memory_space=pltpu.VMEM)
SM = functools.partial(pl.BlockSpec, memory_space=pltpu.SMEM)


def dot(a, b, ca, cb):
    return lax.dot_general(a, b, (((ca,), (cb,)), ((), ())), preferred_element_type=F32)


def shifted(array, axis, by):
    length = lax.axis_size(axis)
    pairs = [(i, i + by) for i in range(length) if 0 <= i + by < length]
    return lax.ppermute(array, axis, pairs)


def locals_kernel(
    xbc_ref, before_ref, w_ref, bias_ref, step_ref, rate_ref, dy_ref,
    zt_ref, bc_ref, dyt_ref, der_ref, cl_ref, s_ref, u_ref, end_ref, xw_ref, dw_ref,
):
    row = lax.broadcasted_iota(jnp.int32, (GROUP, GROUP), 0)
    col = lax.broadcasted_iota(jnp.int32, (GROUP, GROUP), 1)
    upper = (row <= col).astype(F32)
    log_steps = -(step_ref[...] * rate_ref[...])
    cl_ref[...] = jnp.dot(log_steps, upper, precision=HI, preferred_element_type=F32)

    def activate(cols):
        x = xbc_ref[:, cols].astype(F32)
        padded = jnp.concatenate([before_ref[:, cols].astype(F32), x], axis=0)
        pre = bias_ref[:, cols]
        for k in range(KCONV):
            pre = pre + w_ref[k : k + 1, cols] * padded[5 + k : 5 + k + GROUP]
        sig = 1.0 / (1.0 + jnp.exp(-pre))
        der_ref[:, cols] = sig * (1.0 + pre * (1.0 - sig))
        return pre * sig

    @pl.loop(0, XW // TILE)
    def _(i):
        cols = pl.ds(pl.multiple_of(i * TILE, TILE), TILE)
        zt_ref[cols, :] = activate(cols).T.astype(BF16)
        dyt_ref[cols, :] = dy_ref[:, cols].astype(F32).T.astype(BF16)

    tail_z = activate(pl.ds(XW, TILE))
    bc_ref[...] = tail_z.astype(BF16)
    zt_ref[pl.ds(XW, TILE), :] = tail_z.T.astype(BF16)
    cum = cl_ref[...]
    end_ref[...] = jnp.broadcast_to(jnp.exp(cum[:, GROUP - 1 : GROUP]), (HEADS, STATE))

    @pl.loop(0, HEADS)
    def _(h):
        rows = pl.ds(pl.multiple_of(h * HEAD_DIM, HEAD_DIM), HEAD_DIM)
        cl = cl_ref[pl.ds(h, 1), :]
        xw_ref[rows, :] = (
            zt_ref[rows, :].astype(F32) * jnp.exp(cl[:, GROUP - 1 : GROUP] - cl)
        ).astype(BF16)
        dw_ref[rows, :] = (dyt_ref[rows, :].astype(F32) * jnp.exp(cl)).astype(BF16)

    @pl.loop(0, XW // TILE)
    def _(i):
        rows = pl.ds(pl.multiple_of(i * TILE, TILE), TILE)
        s_ref[rows, :] = dot(xw_ref[rows, :], bc_ref[:, :STATE], 1, 0).astype(BF16)
        u_ref[rows, :] = dot(dw_ref[rows, :], bc_ref[:, STATE:], 1, 0).astype(BF16)


def states_kernel(
    s_ref, u_ref, a_ref, start_ref, end_ref,
    sp, up, ap, ein, gin, eout, gout, sout, uout,
    send1, recv1, send2, recv2, send3, recv3, senda, recva,
):
    me = lax.axis_index("seq")
    n = lax.axis_size("seq")
    y = me % 2
    z = me // 2
    nz = n // 2
    pair = me + 1 - 2 * y
    mine = y * HALF
    other = (1 - y) * HALF
    last = nz - 1

    barrier = pltpu.get_barrier_semaphore()
    pl.semaphore_signal(barrier, inc=1, device_id={"seq": pair}, device_id_type=MESH)

    @pl.when(z > 0)
    def _():
        pl.semaphore_signal(barrier, inc=1, device_id={"seq": me - 2}, device_id_type=MESH)

    @pl.when(z < last)
    def _():
        pl.semaphore_signal(barrier, inc=1, device_id={"seq": me + 2}, device_id_type=MESH)

    edge = jnp.where(z > 0, 1, 0) + jnp.where(z < last, 1, 0)
    pl.semaphore_wait(barrier, 1 + edge)

    def send(src, dst, ss, rs, to):
        return pltpu.make_async_remote_copy(
            src_ref=src, dst_ref=dst, send_sem=ss, recv_sem=rs,
            device_id={"seq": to}, device_id_type=MESH,
        )

    def part(c):
        return pl.ds(c * CHUNK, CHUNK)

    def pair_copy(j, c):
        src, dst = ((s_ref, sp), (u_ref, up))[j]
        return send(
            src.at[pl.ds(other + c * CHUNK, CHUNK)], dst.at[part(c)],
            send1.at[j, c], recv1.at[j, c], pair,
        )

    def chain_copy(j, c):
        src, dst = ((eout, ein), (gout, gin))[j]
        return send(
            src.at[part(c)], dst.at[part(c)], send2.at[j, c], recv2.at[j, c],
            me + 2 if j == 0 else me - 2,
        )

    def back_copy(j, c):
        src, dst = ((sout, start_ref), (uout, end_ref))[j]
        return send(
            src.at[part(c)], dst.at[pl.ds(mine + c * CHUNK, CHUNK)],
            send3.at[j, c], recv3.at[j, c], pair,
        )

    decay_copy = send(a_ref, ap, senda, recva, pair)
    decay_copy.start()

    def begin(j):
        @pl.loop(0, NCHUNK)
        def _(c):
            pair_copy(j, c).start()

    def run(j):
        has_in = z > 0 if j == 0 else z < last
        has_out = z < last if j == 0 else z > 0
        inbox, outbox = ((ein, eout), (gin, gout))[j]
        got, own, back, result = ((sp, s_ref, sout, start_ref), (up, u_ref, uout, end_ref))[j]

        @pl.when(jnp.logical_not(has_in))
        def _():
            inbox[...] = jnp.zeros_like(inbox)

        @pl.loop(0, NCHUNK)
        def _(c):
            pair_copy(j, c).wait_recv()
            here = pl.ds(mine + c * CHUNK, CHUNK)
            first = y == 0
            aa = a_ref[here, :][:, None, :]
            bb = ap[here, :][:, None, :]
            a0 = jnp.where(first, aa, bb)
            a1 = jnp.where(first, bb, aa)
            vv = own[here].astype(F32)
            ww = got[part(c)].astype(F32)
            v0 = jnp.where(first, vv, ww)
            v1 = jnp.where(first, ww, vv)

            @pl.when(has_in)
            def _():
                chain_copy(j, c).wait_recv()

            carry = inbox[part(c)].astype(F32)
            if j == 0:
                near, far = carry, a0 * carry + v0
                leave = a1 * far + v1
                kept = jnp.where(first, near, far)
                given = jnp.where(first, far, near)
            else:
                far, near = carry, a1 * carry + v1
                leave = a0 * near + v0
                kept = jnp.where(first, near, far)
                given = jnp.where(first, far, near)
            outbox[part(c)] = leave.astype(BF16)

            @pl.when(has_out)
            def _():
                chain_copy(j, c).start()

            back[part(c)] = given.astype(BF16)
            back_copy(j, c).start()
            result[here] = kept.astype(BF16)

    @pl.when(z < nz - nz // 2)
    def _():
        begin(0)
        begin(1)
        decay_copy.wait_recv()
        run(0)
        run(1)

    @pl.when(z >= nz - nz // 2)
    def _():
        begin(1)
        begin(0)
        decay_copy.wait_recv()
        run(1)
        run(0)

    decay_copy.wait_send()
    for j in range(2):
        @pl.loop(0, NCHUNK)
        def _(c):
            pair_copy(j, c).wait_send()
            back_copy(j, c).wait()

            @pl.when(z < last if j == 0 else z > 0)
            def _():
                chain_copy(j, c).wait_send()


def grads_kernel(
    zt_ref, bc_ref, dyt_ref, der_ref, cl_ref, s_ref, a_ref, xw_ref, dw_ref,
    step_ref, rate_ref, skip_ref, xbc_ref, before_ref, w_ref,
    gin_ref, edge_ref, front_ref, gstep_ref, gw_ref, grate_ref, gskip_ref,
    gz_ref, wsum_ref, d_ref, q_ref, l_ref, k_ref,
):
    row = lax.broadcasted_iota(jnp.int32, (GROUP, GROUP), 0)
    col = lax.broadcasted_iota(jnp.int32, (GROUP, GROUP), 1)
    causal = row >= col
    bproj = bc_ref[:, :STATE]
    cproj = bc_ref[:, STATE:]
    gram = dot(cproj, bproj, 1, 1)
    wsum_ref[...] = jnp.zeros_like(wsum_ref)

    def head(h):
        rows = pl.ds(pl.multiple_of(h * HEAD_DIM, HEAD_DIM), HEAD_DIM)
        xt = zt_ref[rows, :]
        dyt = dyt_ref[rows, :]
        cl = cl_ref[pl.ds(h, 1), :]
        wide = jnp.broadcast_to(cl, (STATE, GROUP)).T
        gap = jnp.concatenate([wide, wide], axis=1) - cl
        decay = jnp.where(causal, jnp.exp(gap), 0.0)
        inner = dot(dyt, xt, 0, 0)
        wsum_ref[...] += decay * inner
        kmat = (decay * gram).astype(BF16)
        intra = dot(dyt, kmat, 1, 0)
        yt = dot(xt, kmat, 1, 1)
        badj = dot(a_ref[rows, :], zt_ref[pl.ds(XW, STATE), :], 1, 0)
        cst = dot(s_ref[rows, :], zt_ref[pl.ds(XW + STATE, STATE), :], 1, 0)
        log_end = cl[:, GROUP - 1 : GROUP]
        tail = jnp.exp(log_end - cl)
        xf = xt.astype(F32)
        dyf = dyt.astype(F32)
        csum = jnp.sum(xf * intra, axis=0, keepdims=True)
        rsum = jnp.sum(dyf * yt, axis=0, keepdims=True)
        rterm = tail * jnp.sum(xf * badj, axis=0, keepdims=True)
        qterm = jnp.exp(cl) * jnp.sum(dyf * cst, axis=0, keepdims=True)
        prod = a_ref[rows, :].astype(F32) * s_ref[rows, :].astype(F32)
        four = jnp.exp(log_end) * jnp.sum(jnp.sum(prod, axis=0, keepdims=True), axis=1, keepdims=True)
        one = pl.ds(h, 1)
        gain = csum - rsum + rterm
        d_ref[one, :] = gain
        q_ref[one, :] = qterm
        l_ref[one, :] = four - gain
        k_ref[one, :] = jnp.sum(xf * dyf, axis=0, keepdims=True)
        return intra + tail * badj + skip_ref[h] * dyf

    @pl.loop(0, HEADS // 2)
    def _(hp):
        both = jnp.concatenate([head(2 * hp), head(2 * hp + 1)], axis=0)
        gz_ref[:, pl.ds(pl.multiple_of(hp * STATE, STATE), STATE)] = both.T

    wlow = wsum_ref[...].astype(BF16)
    gb = dot(wlow, cproj, 0, 0) + dot(a_ref[...], xw_ref[...], 0, 0).T
    gc = dot(wlow, bproj, 1, 0) + dot(s_ref[...], dw_ref[...], 0, 0).T
    gz_ref[:, pl.ds(XW, STATE)] = gb
    gz_ref[:, pl.ds(XW + STATE, STATE)] = gc
    upper = (row <= col).astype(F32)
    lower = (row >= col).astype(F32)
    glog = jnp.dot(d_ref[...], upper, precision=HI, preferred_element_type=F32)
    glog = glog + jnp.dot(q_ref[...], lower, precision=HI, preferred_element_type=F32)
    glog = glog + l_ref[...]
    gstep_ref[...] = -rate_ref[...] * glog
    grate_ref[...] = -jnp.sum(step_ref[...] * glog, axis=1, keepdims=True)
    gskip_ref[...] = jnp.sum(k_ref[...], axis=1, keepdims=True)

    @pl.loop(0, CH // TILE)
    def _(i):
        cols = pl.ds(pl.multiple_of(i * TILE, TILE), TILE)
        gp = gz_ref[:, cols] * der_ref[:, cols]
        padded = jnp.concatenate([gp, jnp.zeros((8, TILE), F32)], axis=0)
        gin = w_ref[KCONV - 1 : KCONV, cols] * gp
        for k in range(KCONV - 1):
            off = KCONV - 1 - k
            gin = gin + w_ref[k : k + 1, cols] * padded[off : off + GROUP]
        gin_ref[:, cols] = gin.astype(BF16)
        edge_ref[:, cols] = gin[GROUP - 8 :]
        first = gp[:8]
        sub = lax.broadcasted_iota(jnp.int32, (8, TILE), 0)
        front_pad = jnp.concatenate([jnp.zeros((8, TILE), F32), first], axis=0)
        rim = jnp.zeros((8, TILE), F32)
        for k in range(KCONV - 1):
            off = KCONV - 1 - k
            piece = jnp.where(sub >= 8 - off, front_pad[off : off + 8], 0.0)
            rim = rim + w_ref[k : k + 1, cols] * piece
        front_ref[:, cols] = rim
        x = jnp.concatenate([before_ref[:, cols].astype(F32), xbc_ref[:, cols].astype(F32)], axis=0)
        for k in range(KCONV):
            gw_ref[k : k + 1, cols] = jnp.sum(gp * x[5 + k : 5 + k + GROUP], axis=0, keepdims=True)
        gw_ref[KCONV : KCONV + 1, cols] = jnp.sum(gp, axis=0, keepdims=True)


def bits_of(n):
    out = []
    b = 1
    while b < n:
        out.append(b)
        b *= 2
    return out


def reduce_kernel(steps, pack_ref, front_ref, out_ref, rim_ref, acc, box, ssem, rsem, fs, fr):
    pos = {"dp": lax.axis_index("dp"), "seq": lax.axis_index("seq")}
    n = lax.axis_size("seq")
    me = pos["seq"]
    to = []
    for axis, b in steps:
        p = pos[axis]
        to.append({axis: p + b * (1 - 2 * ((p // b) % 2))})
    barrier = pltpu.get_barrier_semaphore()
    for where in to:
        pl.semaphore_signal(barrier, inc=1, device_id=where, device_id_type=MESH)

    @pl.when(me > 0)
    def _():
        pl.semaphore_signal(barrier, inc=1, device_id={"seq": me - 1}, device_id_type=MESH)

    @pl.when(me < n - 1)
    def _():
        pl.semaphore_signal(barrier, inc=1, device_id={"seq": me + 1}, device_id_type=MESH)

    edge = jnp.where(me > 0, 1, 0) + jnp.where(me < n - 1, 1, 0)
    pl.semaphore_wait(barrier, len(to) + edge)

    rim = pltpu.make_async_remote_copy(
        src_ref=front_ref, dst_ref=rim_ref, send_sem=fs, recv_sem=fr,
        device_id={"seq": me - 1}, device_id_type=MESH,
    )

    @pl.when(me > 0)
    def _():
        rim.start()

    copies = []
    for i, where in enumerate(to):
        copy = pltpu.make_async_remote_copy(
            src_ref=pack_ref if i == 0 else acc.at[i], dst_ref=box.at[i],
            send_sem=ssem.at[i], recv_sem=rsem.at[i],
            device_id=where, device_id_type=MESH,
        )
        copy.start()
        copies.append(copy)
        copy.wait_recv()
        total = (pack_ref[...] if i == 0 else acc[i]) + box[i]
        if i + 1 < len(to):
            acc[i + 1] = total
        else:
            out_ref[...] = total
    for copy in copies:
        copy.wait_send()

    @pl.when(me > 0)
    def _():
        rim.wait_send()

    @pl.when(me < n - 1)
    def _():
        rim.wait_recv()

    @pl.when(me == n - 1)
    def _():
        rim_ref[...] = jnp.zeros_like(rim_ref)


def sds(shape, dtype):
    return jax.ShapeDtypeStruct(shape, dtype)


LIMIT = 60 * 1024 * 1024


def shards(xbc_in, conv_weight, conv_bias, step_sizes, decay_rates, skip_gain, grad_out):
    rim_len = KCONV - 1
    tokens = xbc_in.shape[1]
    before = shifted(xbc_in[:, tokens - 8 :, :], "seq", 1)[0]
    xbc = xbc_in[0]
    dy = grad_out[0]
    step = step_sizes[0]
    rate = decay_rates[:, None]
    state = (HEADS, HEAD_DIM, STATE)
    zt, bc, dyt, der, cl, s, u, decay, xw, dw = pl.pallas_call(
        locals_kernel,
        out_shape=[
            sds((CH, GROUP), BF16), sds((GROUP, 2 * STATE), BF16), sds((XW, GROUP), BF16),
            sds((GROUP, CH), F32), sds((HEADS, GROUP), F32), sds((XW, STATE), BF16),
            sds((XW, STATE), BF16), sds((HEADS, STATE), F32), sds((XW, GROUP), BF16),
            sds((XW, GROUP), BF16),
        ],
        in_specs=[VM()] * 7,
        out_specs=[VM()] * 10,
        compiler_params=pltpu.CompilerParams(vmem_limit_bytes=LIMIT),
    )(xbc, before, conv_weight, conv_bias[None], step, rate, dy)

    half = (HALF, HEAD_DIM, STATE)
    dma = pltpu.SemaphoreType.DMA
    start, end = pl.pallas_call(
        states_kernel,
        out_shape=[sds(state, BF16)] * 2,
        in_specs=[VM()] * 3,
        out_specs=[VM()] * 2,
        scratch_shapes=[pltpu.VMEM(half, BF16)] * 2
        + [pltpu.VMEM((HEADS, STATE), F32)]
        + [pltpu.VMEM(half, BF16)] * 6
        + [dma((2, NCHUNK))] * 6
        + [dma, dma],
        compiler_params=pltpu.CompilerParams(
            vmem_limit_bytes=LIMIT, collective_id=0, has_side_effects=True
        ),
    )(s.reshape(state), u.reshape(state), decay)

    gin, edge, front, gstep, gw, grate, gskip = pl.pallas_call(
        grads_kernel,
        out_shape=[
            sds((GROUP, CH), BF16), sds((8, CH), F32), sds((8, CH), F32), sds((HEADS, GROUP), F32),
            sds((KCONV + 1, CH), F32), sds((HEADS, 1), F32), sds((HEADS, 1), F32),
        ],
        in_specs=[VM()] * 11 + [SM()] + [VM()] * 3,
        out_specs=[VM()] * 7,
        scratch_shapes=[pltpu.VMEM((GROUP, CH), F32), pltpu.VMEM((GROUP, GROUP), F32)]
        + [pltpu.VMEM((HEADS, GROUP), F32)] * 4,
        compiler_params=pltpu.CompilerParams(vmem_limit_bytes=LIMIT),
    )(
        zt, bc, dyt, der, cl, start.reshape(XW, STATE), end.reshape(XW, STATE), xw, dw,
        step, rate, skip_gain, xbc, before, conv_weight,
    )

    small = jnp.concatenate([grate[:, 0], gskip[:, 0], jnp.zeros((CH - 2 * HEADS,), F32)])
    pack = jnp.concatenate([gw, small[None], jnp.zeros((2, CH), F32)], axis=0)
    steps = [("dp", b) for b in bits_of(lax.axis_size("dp"))]
    steps += [("seq", b) for b in bits_of(lax.axis_size("seq"))]
    count = len(steps)
    total, rim = pl.pallas_call(
        functools.partial(reduce_kernel, steps),
        out_shape=[sds((8, CH), F32)] * 2,
        in_specs=[VM()] * 2,
        out_specs=[VM()] * 2,
        scratch_shapes=[pltpu.VMEM((count, 8, CH), F32)] * 2 + [dma((count,))] * 2 + [dma, dma],
        compiler_params=pltpu.CompilerParams(
            vmem_limit_bytes=LIMIT, collective_id=1, has_side_effects=True
        ),
    )(pack, front)
    final = (edge + rim).astype(BF16)
    grad_in = lax.dynamic_update_slice(gin, final, (tokens - 8, 0))
    return (
        grad_in[None], gstep[None], total[:KCONV], total[KCONV],
        total[KCONV + 1, :HEADS], total[KCONV + 1, HEADS : 2 * HEADS],
    )


def solution(mesh):
    return jax.shard_map(
        shards,
        mesh=mesh,
        in_specs=(
            P("dp", "seq", None), P(), P(), P("dp", None, "seq"), P(), P(), P("dp", "seq", None),
        ),
        out_specs=(P("dp", "seq", None), P("dp", None, "seq"), P(), P(), P(), P()),
        check_vma=False,
    )
```

```python
import functools
import jax
import jax.numpy as jnp
from jax import lax
from jax.experimental import pallas as pl
from jax.experimental.pallas import tpu as pltpu
from jax.sharding import PartitionSpec as P

HEADS = 40
HEAD_DIM = 64
STATE = 128
GROUP = 256
KCONV = 4
XW = HEADS * HEAD_DIM
CH = XW + 2 * STATE
TILE = 256
HALF = HEADS // 2
CHUNK = 5
EDGE = 16
LINES = CH // TILE
PACK = (KCONV + 1) * LINES + 1
NCHUNK = HALF // CHUNK
MESH = pl.DeviceIdType.MESH
F32 = jnp.float32
BF16 = jnp.bfloat16
HI = lax.Precision.HIGHEST
VM = functools.partial(pl.BlockSpec, memory_space=pltpu.VMEM)
SM = functools.partial(pl.BlockSpec, memory_space=pltpu.SMEM)


def dot(a, b, ca, cb):
    return lax.dot_general(a, b, (((ca,), (cb,)), ((), ())), preferred_element_type=F32)


def shifted(array, axis, by):
    length = lax.axis_size(axis)
    pairs = [(i, i + by) for i in range(length) if 0 <= i + by < length]
    return lax.ppermute(array, axis, pairs)


def locals_kernel(
    xbc_ref, before_ref, w_ref, bias_ref, step_ref, rate_ref, dy_ref,
    zt_ref, bc_ref, dyt_ref, der_ref, cl_ref, s_ref, u_ref, end_ref, xw_ref, dw_ref,
    log_ref,
):
    row = lax.broadcasted_iota(jnp.int32, (GROUP, GROUP), 0)
    col = lax.broadcasted_iota(jnp.int32, (GROUP, GROUP), 1)
    upper = (row <= col).astype(F32)

    @pl.loop(0, HEADS)
    def _(h):
        one = pl.ds(h, 1)
        log_ref[one, :] = -(step_ref[one, :] * rate_ref[h])

    cl_ref[...] = jnp.dot(log_ref[...], upper, precision=HI, preferred_element_type=F32)

    def activate(cols):
        x = xbc_ref[:, cols].astype(F32)
        padded = jnp.concatenate([before_ref[:, cols].astype(F32), x], axis=0)
        pre = bias_ref[cols][None, :]
        for k in range(KCONV):
            pre = pre + w_ref[k : k + 1, cols] * padded[5 + k : 5 + k + GROUP]
        sig = 1.0 / (1.0 + jnp.exp(-pre))
        der_ref[:, cols] = sig * (1.0 + pre * (1.0 - sig))
        return pre * sig

    @pl.loop(0, XW // TILE)
    def _(i):
        cols = pl.ds(pl.multiple_of(i * TILE, TILE), TILE)
        zt_ref[cols, :] = activate(cols).T.astype(BF16)
        dyt_ref[cols, :] = dy_ref[:, cols].astype(F32).T.astype(BF16)

    tail_z = activate(pl.ds(XW, TILE))
    bc_ref[...] = tail_z.astype(BF16)
    zt_ref[pl.ds(XW, TILE), :] = tail_z.T.astype(BF16)
    cum = cl_ref[...]
    end_ref[...] = jnp.broadcast_to(jnp.exp(cum[:, GROUP - 1 : GROUP]), (HEADS, STATE))

    @pl.loop(0, HEADS)
    def _(h):
        rows = pl.ds(pl.multiple_of(h * HEAD_DIM, HEAD_DIM), HEAD_DIM)
        cl = cl_ref[pl.ds(h, 1), :]
        xw_ref[rows, :] = (
            zt_ref[rows, :].astype(F32) * jnp.exp(cl[:, GROUP - 1 : GROUP] - cl)
        ).astype(BF16)
        dw_ref[rows, :] = (dyt_ref[rows, :].astype(F32) * jnp.exp(cl)).astype(BF16)

    @pl.loop(0, XW // TILE)
    def _(i):
        rows = pl.ds(pl.multiple_of(i * TILE, TILE), TILE)
        s_ref[rows, :] = dot(xw_ref[rows, :], bc_ref[:, :STATE], 1, 0).astype(BF16)
        u_ref[rows, :] = dot(dw_ref[rows, :], bc_ref[:, STATE:], 1, 0).astype(BF16)


def states_kernel(
    s_ref, u_ref, a_ref, start_ref, end_ref,
    sp, up, ap, ein, gin, eout, gout, sout, uout,
    send1, recv1, send2, recv2, send3, recv3, senda, recva,
):
    me = lax.axis_index("seq")
    n = lax.axis_size("seq")
    y = me % 2
    z = me // 2
    nz = n // 2
    pair = me + 1 - 2 * y
    mine = y * HALF
    other = (1 - y) * HALF
    last = nz - 1

    barrier = pltpu.get_barrier_semaphore()
    pl.semaphore_signal(barrier, inc=1, device_id={"seq": pair}, device_id_type=MESH)

    @pl.when(z > 0)
    def _():
        pl.semaphore_signal(barrier, inc=1, device_id={"seq": me - 2}, device_id_type=MESH)

    @pl.when(z < last)
    def _():
        pl.semaphore_signal(barrier, inc=1, device_id={"seq": me + 2}, device_id_type=MESH)

    edge = jnp.where(z > 0, 1, 0) + jnp.where(z < last, 1, 0)
    pl.semaphore_wait(barrier, 1 + edge)

    def send(src, dst, ss, rs, to):
        return pltpu.make_async_remote_copy(
            src_ref=src, dst_ref=dst, send_sem=ss, recv_sem=rs,
            device_id={"seq": to}, device_id_type=MESH,
        )

    def part(c):
        return pl.ds(c * CHUNK, CHUNK)

    def pair_copy(j, c):
        src, dst = ((s_ref, sp), (u_ref, up))[j]
        return send(
            src.at[pl.ds(other + c * CHUNK, CHUNK)], dst.at[part(c)],
            send1.at[j, c], recv1.at[j, c], pair,
        )

    def chain_copy(j, c):
        src, dst = ((eout, ein), (gout, gin))[j]
        return send(
            src.at[part(c)], dst.at[part(c)], send2.at[j, c], recv2.at[j, c],
            me + 2 if j == 0 else me - 2,
        )

    def back_copy(j, c):
        src, dst = ((sout, start_ref), (uout, end_ref))[j]
        return send(
            src.at[part(c)], dst.at[pl.ds(mine + c * CHUNK, CHUNK)],
            send3.at[j, c], recv3.at[j, c], pair,
        )

    decay_copy = send(a_ref, ap, senda, recva, pair)
    decay_copy.start()

    def begin(j):
        @pl.loop(0, NCHUNK)
        def _(c):
            pair_copy(j, c).start()

    def run(j):
        has_in = z > 0 if j == 0 else z < last
        has_out = z < last if j == 0 else z > 0
        inbox, outbox = ((ein, eout), (gin, gout))[j]
        got, own, back, result = ((sp, s_ref, sout, start_ref), (up, u_ref, uout, end_ref))[j]

        @pl.when(jnp.logical_not(has_in))
        def _():
            inbox[...] = jnp.zeros_like(inbox)

        @pl.loop(0, NCHUNK)
        def _(c):
            pair_copy(j, c).wait_recv()
            here = pl.ds(mine + c * CHUNK, CHUNK)
            first = y == 0
            aa = a_ref[here, :][:, None, :]
            bb = ap[here, :][:, None, :]
            a0 = jnp.where(first, aa, bb)
            a1 = jnp.where(first, bb, aa)
            vv = own[here].astype(F32)
            ww = got[part(c)].astype(F32)
            v0 = jnp.where(first, vv, ww)
            v1 = jnp.where(first, ww, vv)

            @pl.when(has_in)
            def _():
                chain_copy(j, c).wait_recv()

            carry = inbox[part(c)].astype(F32)
            if j == 0:
                near, far = carry, a0 * carry + v0
                leave = a1 * far + v1
                kept = jnp.where(first, near, far)
                given = jnp.where(first, far, near)
            else:
                far, near = carry, a1 * carry + v1
                leave = a0 * near + v0
                kept = jnp.where(first, near, far)
                given = jnp.where(first, far, near)
            outbox[part(c)] = leave.astype(BF16)

            @pl.when(has_out)
            def _():
                chain_copy(j, c).start()

            back[part(c)] = given.astype(BF16)
            back_copy(j, c).start()
            result[here] = kept.astype(BF16)

    @pl.when(z < nz - nz // 2)
    def _():
        begin(0)
        begin(1)
        decay_copy.wait_recv()
        run(0)
        run(1)

    @pl.when(z >= nz - nz // 2)
    def _():
        begin(1)
        begin(0)
        decay_copy.wait_recv()
        run(1)
        run(0)

    decay_copy.wait_send()
    for j in range(2):
        @pl.loop(0, NCHUNK)
        def _(c):
            pair_copy(j, c).wait_send()
            back_copy(j, c).wait()

            @pl.when(z < last if j == 0 else z > 0)
            def _():
                chain_copy(j, c).wait_send()


def grads_kernel(
    zt_ref, bc_ref, dyt_ref, der_ref, cl_ref, s_ref, a_ref, xw_ref, dw_ref,
    step_ref, rate_ref, skip_ref, xbc_ref, before_ref, w_ref,
    gin_ref, edge_ref, front_ref, gstep_ref, pack_ref,
    gz_ref, wsum_ref, d_ref, q_ref, l_ref, k_ref,
):
    row = lax.broadcasted_iota(jnp.int32, (GROUP, GROUP), 0)
    col = lax.broadcasted_iota(jnp.int32, (GROUP, GROUP), 1)
    causal = row >= col
    bproj = bc_ref[:, :STATE]
    cproj = bc_ref[:, STATE:]
    gram = dot(cproj, bproj, 1, 1)
    wsum_ref[...] = jnp.zeros_like(wsum_ref)

    def head(h):
        rows = pl.ds(pl.multiple_of(h * HEAD_DIM, HEAD_DIM), HEAD_DIM)
        xt = zt_ref[rows, :]
        dyt = dyt_ref[rows, :]
        cl = cl_ref[pl.ds(h, 1), :]
        wide = jnp.broadcast_to(cl, (STATE, GROUP)).T
        gap = jnp.concatenate([wide, wide], axis=1) - cl
        decay = jnp.where(causal, jnp.exp(gap), 0.0)
        inner = dot(dyt, xt, 0, 0)
        wsum_ref[...] += decay * inner
        kmat = (decay * gram).astype(BF16)
        intra = dot(dyt, kmat, 1, 0)
        yt = dot(xt, kmat, 1, 1)
        badj = dot(a_ref[rows, :], zt_ref[pl.ds(XW, STATE), :], 1, 0)
        cst = dot(s_ref[rows, :], zt_ref[pl.ds(XW + STATE, STATE), :], 1, 0)
        log_end = cl[:, GROUP - 1 : GROUP]
        tail = jnp.exp(log_end - cl)
        xf = xt.astype(F32)
        dyf = dyt.astype(F32)
        csum = jnp.sum(xf * intra, axis=0, keepdims=True)
        rsum = jnp.sum(dyf * yt, axis=0, keepdims=True)
        rterm = tail * jnp.sum(xf * badj, axis=0, keepdims=True)
        qterm = jnp.exp(cl) * jnp.sum(dyf * cst, axis=0, keepdims=True)
        prod = a_ref[rows, :].astype(F32) * s_ref[rows, :].astype(F32)
        four = jnp.exp(log_end) * jnp.sum(jnp.sum(prod, axis=0, keepdims=True), axis=1, keepdims=True)
        one = pl.ds(h, 1)
        gain = csum - rsum + rterm
        d_ref[one, :] = gain
        q_ref[one, :] = qterm
        l_ref[one, :] = four - gain
        k_ref[one, :] = jnp.sum(xf * dyf, axis=0, keepdims=True)
        return intra + tail * badj + skip_ref[h] * dyf

    @pl.loop(0, HEADS // 2)
    def _(hp):
        both = jnp.concatenate([head(2 * hp), head(2 * hp + 1)], axis=0)
        gz_ref[:, pl.ds(pl.multiple_of(hp * STATE, STATE), STATE)] = both.T

    wlow = wsum_ref[...].astype(BF16)
    gb = dot(wlow, cproj, 0, 0) + dot(a_ref[...], xw_ref[...], 0, 0).T
    gc = dot(wlow, bproj, 1, 0) + dot(s_ref[...], dw_ref[...], 0, 0).T
    gz_ref[:, pl.ds(XW, STATE)] = gb
    gz_ref[:, pl.ds(XW + STATE, STATE)] = gc
    upper = (row <= col).astype(F32)
    lower = (row >= col).astype(F32)
    glog = jnp.dot(d_ref[...], upper, precision=HI, preferred_element_type=F32)
    glog = glog + jnp.dot(q_ref[...], lower, precision=HI, preferred_element_type=F32)
    glog = glog + l_ref[...]
    d_ref[...] = glog

    @pl.loop(0, HEADS)
    def _(h):
        one = pl.ds(h, 1)
        gstep_ref[one, :] = -(d_ref[one, :] * rate_ref[h])

    ones = jnp.ones((8, GROUP), F32)
    sums = (-step_ref[...] * glog, k_ref[...])
    for c in range(2):
        line = lax.dot_general(
            ones, sums[c], (((1,), (1,)), ((), ())), precision=HI, preferred_element_type=F32
        )
        line = jnp.concatenate([line[:1], jnp.zeros((1, STATE - HEADS), F32)], axis=1)
        pack_ref[c, PACK - 1 : PACK, :] = line

    @pl.loop(0, CH // TILE)
    def _(i):
        cols = pl.ds(pl.multiple_of(i * TILE, TILE), TILE)
        gp = gz_ref[:, cols] * der_ref[:, cols]
        padded = jnp.concatenate([gp, jnp.zeros((8, TILE), F32)], axis=0)
        gin = w_ref[KCONV - 1 : KCONV, cols] * gp
        for k in range(KCONV - 1):
            off = KCONV - 1 - k
            gin = gin + w_ref[k : k + 1, cols] * padded[off : off + GROUP]
        gin_ref[:, cols] = gin.astype(BF16)
        edge_ref[:, cols] = gin[GROUP - EDGE :]
        first = gp[:8]
        sub = lax.broadcasted_iota(jnp.int32, (8, TILE), 0)
        front_pad = jnp.concatenate([jnp.zeros((8, TILE), F32), first], axis=0)
        rim = jnp.zeros((8, TILE), F32)
        for k in range(KCONV - 1):
            off = KCONV - 1 - k
            piece = jnp.where(sub >= 8 - off, front_pad[off : off + 8], 0.0)
            rim = rim + w_ref[k : k + 1, cols] * piece
        front_ref[:, cols] = rim
        x = jnp.concatenate([before_ref[:, cols].astype(F32), xbc_ref[:, cols].astype(F32)], axis=0)
        for k in range(KCONV + 1):
            terms = gp * x[5 + k : 5 + k + GROUP] if k < KCONV else gp
            line = jnp.sum(terms, axis=0, keepdims=True)
            for c in range(2):
                pack_ref[c, pl.ds(k * LINES + i, 1), :] = line[:, c * STATE : (c + 1) * STATE]


def bits_of(n):
    out = []
    b = 1
    while b < n:
        out.append(b)
        b *= 2
    return out


def reduce_kernel(steps, pack_ref, front_ref, out_ref, rim_ref, acc, box, ssem, rsem, fs, fr, gs, gr):
    pos = {"dp": lax.axis_index("dp"), "seq": lax.axis_index("seq")}
    n = lax.axis_size("seq")
    me = pos["seq"]
    core = pos["dp"] % 2
    to = []
    for axis, b in steps:
        p = pos[axis]
        to.append({axis: p + b * (1 - 2 * ((p // b) % 2))})
    barrier = pltpu.get_barrier_semaphore()
    for where in to:
        pl.semaphore_signal(barrier, inc=1, device_id=where, device_id_type=MESH)

    @pl.when(me > 0)
    def _():
        pl.semaphore_signal(barrier, inc=1, device_id={"seq": me - 1}, device_id_type=MESH)

    @pl.when(me < n - 1)
    def _():
        pl.semaphore_signal(barrier, inc=1, device_id={"seq": me + 1}, device_id_type=MESH)

    edge = jnp.where(me > 0, 1, 0) + jnp.where(me < n - 1, 1, 0)
    pl.semaphore_wait(barrier, len(to) + edge)

    rim = pltpu.make_async_remote_copy(
        src_ref=front_ref, dst_ref=rim_ref, send_sem=fs, recv_sem=fr,
        device_id={"seq": me - 1}, device_id_type=MESH,
    )

    @pl.when(me > 0)
    def _():
        rim.start()

    copies = []
    for i, where in enumerate(to):
        copy = pltpu.make_async_remote_copy(
            src_ref=pack_ref.at[1 - core] if i == 0 else acc.at[i], dst_ref=box.at[i],
            send_sem=ssem.at[i], recv_sem=rsem.at[i],
            device_id=where, device_id_type=MESH,
        )
        copy.start()
        copies.append(copy)
        copy.wait_recv()
        total = (pack_ref[core] if i == 0 else acc[i]) + box[i]
        acc[i + 1] = total
    share = pltpu.make_async_remote_copy(
        src_ref=acc.at[len(to)], dst_ref=out_ref.at[core], send_sem=gs, recv_sem=gr,
        device_id=to[0], device_id_type=MESH,
    )
    share.start()
    out_ref[core] = total
    share.wait()
    for copy in copies:
        copy.wait_send()

    @pl.when(me > 0)
    def _():
        rim.wait_send()

    @pl.when(me < n - 1)
    def _():
        rim.wait_recv()

    @pl.when(me == n - 1)
    def _():
        rim_ref[...] = jnp.zeros_like(rim_ref)


def finish_kernel(
    total_ref, edge_ref, rim_ref, gin_ref, out_ref, gw_ref, gb_ref, grate_ref, gskip_ref, last, sem
):
    final = edge_ref[...] + jnp.concatenate([jnp.zeros((8, CH), F32), rim_ref[...]], axis=0)
    last[...] = final.astype(BF16)
    copy = pltpu.make_async_copy(last, out_ref.at[pl.ds(GROUP - EDGE, EDGE)], sem)
    copy.start()
    for i in range(LINES):
        for c in range(2):
            cols = pl.ds((2 * i + c) * STATE, STATE)
            for k in range(KCONV):
                gw_ref[k : k + 1, cols] = total_ref[c, pl.ds(k * LINES + i, 1), :]
            gb_ref[cols] = total_ref[c, KCONV * LINES + i, :]
    grate_ref[...] = total_ref[0, PACK - 1, :HEADS]
    gskip_ref[...] = total_ref[1, PACK - 1, :HEADS]
    copy.wait()


def sds(shape, dtype):
    return jax.ShapeDtypeStruct(shape, dtype)


LIMIT = 60 * 1024 * 1024


def shards(xbc_in, conv_weight, conv_bias, step_sizes, decay_rates, skip_gain, grad_out):
    rim_len = KCONV - 1
    tokens = xbc_in.shape[1]
    before = shifted(xbc_in[:, tokens - 8 :, :], "seq", 1)[0]
    xbc = xbc_in[0]
    dy = grad_out[0]
    step = step_sizes[0]
    state = (HEADS, HEAD_DIM, STATE)
    zt, bc, dyt, der, cl, s, u, decay, xw, dw = pl.pallas_call(
        locals_kernel,
        out_shape=[
            sds((CH, GROUP), BF16), sds((GROUP, 2 * STATE), BF16), sds((XW, GROUP), BF16),
            sds((GROUP, CH), F32), sds((HEADS, GROUP), F32), sds((XW, STATE), BF16),
            sds((XW, STATE), BF16), sds((HEADS, STATE), F32), sds((XW, GROUP), BF16),
            sds((XW, GROUP), BF16),
        ],
        in_specs=[VM()] * 5 + [SM(), VM()],
        out_specs=[VM()] * 10,
        scratch_shapes=[pltpu.VMEM((HEADS, GROUP), F32)],
        compiler_params=pltpu.CompilerParams(vmem_limit_bytes=LIMIT),
    )(xbc, before, conv_weight, conv_bias, step, decay_rates, dy)

    half = (HALF, HEAD_DIM, STATE)
    dma = pltpu.SemaphoreType.DMA
    start, end = pl.pallas_call(
        states_kernel,
        out_shape=[sds(state, BF16)] * 2,
        in_specs=[VM()] * 3,
        out_specs=[VM()] * 2,
        scratch_shapes=[pltpu.VMEM(half, BF16)] * 2
        + [pltpu.VMEM((HEADS, STATE), F32)]
        + [pltpu.VMEM(half, BF16)] * 6
        + [dma((2, NCHUNK))] * 6
        + [dma, dma],
        compiler_params=pltpu.CompilerParams(
            vmem_limit_bytes=LIMIT, collective_id=0, has_side_effects=True
        ),
    )(s.reshape(state), u.reshape(state), decay)

    gin, edge, front, gstep, pack = pl.pallas_call(
        grads_kernel,
        out_shape=[
            sds((GROUP, CH), BF16), sds((EDGE, CH), F32), sds((8, CH), F32), sds((HEADS, GROUP), F32),
            sds((2, PACK, STATE), F32),
        ],
        in_specs=[VM()] * 10 + [SM()] * 2 + [VM()] * 3,
        out_specs=[VM()] * 5,
        scratch_shapes=[pltpu.VMEM((GROUP, CH), F32), pltpu.VMEM((GROUP, GROUP), F32)]
        + [pltpu.VMEM((HEADS, GROUP), F32)] * 4,
        compiler_params=pltpu.CompilerParams(vmem_limit_bytes=LIMIT),
    )(
        zt, bc, dyt, der, cl, start.reshape(XW, STATE), end.reshape(XW, STATE), xw, dw,
        step, decay_rates, skip_gain, xbc, before, conv_weight,
    )

    steps = [("dp", b) for b in bits_of(lax.axis_size("dp"))]
    steps += [("seq", b) for b in bits_of(lax.axis_size("seq"))]
    count = len(steps)
    total, rim = pl.pallas_call(
        functools.partial(reduce_kernel, steps),
        out_shape=[sds((2, PACK, STATE), F32), sds((8, CH), F32)],
        in_specs=[VM()] * 2,
        out_specs=[VM()] * 2,
        scratch_shapes=[pltpu.VMEM((count + 1, PACK, STATE), F32)] * 2
        + [dma((count,))] * 2
        + [dma] * 4,
        compiler_params=pltpu.CompilerParams(
            vmem_limit_bytes=LIMIT, collective_id=1, has_side_effects=True
        ),
    )(pack, front)
    grad_in, gw, gb, grate, gskip = pl.pallas_call(
        finish_kernel,
        out_shape=[
            sds((GROUP, CH), BF16), sds((KCONV, CH), F32), sds((CH,), F32),
            sds((HEADS,), F32), sds((HEADS,), F32),
        ],
        in_specs=[VM()] * 3 + [pl.BlockSpec(memory_space=pl.ANY)],
        out_specs=[pl.BlockSpec(memory_space=pl.ANY)] + [VM()] * 4,
        scratch_shapes=[pltpu.VMEM((EDGE, CH), BF16), dma],
        input_output_aliases={3: 0},
    )(total, edge, rim, gin)
    return (grad_in[None], gstep[None], gw, gb, grate, gskip)


def solution(mesh):
    return jax.shard_map(
        shards,
        mesh=mesh,
        in_specs=(
            P("dp", "seq", None), P(), P(), P("dp", None, "seq"), P(), P(), P("dp", "seq", None),
        ),
        out_specs=(P("dp", "seq", None), P("dp", None, "seq"), P(), P(), P(), P()),
        check_vma=False,
    )
```

```python
import functools
import jax
import jax.numpy as jnp
from jax import lax
from jax.experimental import pallas as pl
from jax.experimental.pallas import tpu as pltpu
from jax.sharding import PartitionSpec as P

HEADS = 40
HEAD_DIM = 64
STATE = 128
GROUP = 256
KCONV = 4
XW = HEADS * HEAD_DIM
CH = XW + 2 * STATE
TILE = 256
HALF = HEADS // 2
CHUNK = 5
EDGE = 16
LINES = CH // TILE
PACK = (KCONV + 1) * LINES + 1
NCHUNK = HALF // CHUNK
MESH = pl.DeviceIdType.MESH
F32 = jnp.float32
BF16 = jnp.bfloat16
HI = lax.Precision.HIGHEST
VM = functools.partial(pl.BlockSpec, memory_space=pltpu.VMEM)
SM = functools.partial(pl.BlockSpec, memory_space=pltpu.SMEM)


def dot(a, b, ca, cb):
    return lax.dot_general(a, b, (((ca,), (cb,)), ((), ())), preferred_element_type=F32)


def bits_of(n):
    out = []
    b = 1
    while b < n:
        out.append(b)
        b *= 2
    return out


def core_kernel(
    steps,
    xbc_ref, w_ref, bias_ref, step_ref, rate_ref, dy_ref, skip_ref,
    gin_ref, edge_ref, gstep_ref, out_ref, rim_ref,
    zt_ref, bc_ref, dyt_ref, der_ref, cl_ref, xw_ref, dw_ref, log_ref, before_ref,
    s_ref, u_ref, dec_ref, start_ref, end_ref,
    sp, up, ap, ein, gin, eout, gout, sout, uout,
    gram_ref, wsum_ref, intra_ref, gz_ref, d_ref, q_ref, l_ref, k_ref, front_ref, pack_ref,
    acc, box,
    send1, recv1, send2, recv2, send3, recv3, senda, recva,
    ssem, rsem, fs, fr, gs, gr, bs, br,
):
    pos = {"dp": lax.axis_index("dp"), "seq": lax.axis_index("seq")}
    me = pos["seq"]
    n = lax.axis_size("seq")
    core = pos["dp"] % 2
    y = me % 2
    z = me // 2
    nz = n // 2
    pair = me + 1 - 2 * y
    mine = y * HALF
    other = (1 - y) * HALF
    last = nz - 1
    low = z < nz - nz // 2
    to = []
    for axis, b in steps:
        p = pos[axis]
        to.append({axis: p + b * (1 - 2 * ((p // b) % 2))})
    barrier = pltpu.get_barrier_semaphore()
    for where in to + [{"seq": pair}]:
        pl.semaphore_signal(barrier, inc=1, device_id=where, device_id_type=MESH)
    edges = 0
    for by in (-2, -1, 1, 2):
        inside = me + by >= 0 if by < 0 else me + by < n
        edges = edges + jnp.where(inside, 1, 0)

        @pl.when(inside)
        def _():
            pl.semaphore_signal(barrier, inc=1, device_id={"seq": me + by}, device_id_type=MESH)

    pl.semaphore_wait(barrier, len(to) + 1 + edges)

    rim_in = pltpu.make_async_remote_copy(
        src_ref=xbc_ref.at[pl.ds(GROUP - 8, 8)], dst_ref=before_ref, send_sem=bs, recv_sem=br,
        device_id={"seq": me + 1}, device_id_type=MESH,
    )

    @pl.when(me < n - 1)
    def _():
        rim_in.start()

    row = lax.broadcasted_iota(jnp.int32, (GROUP, GROUP), 0)
    col = lax.broadcasted_iota(jnp.int32, (GROUP, GROUP), 1)
    causal = row >= col
    upper = (row <= col).astype(F32)

    @pl.loop(0, HEADS)
    def _(h):
        one = pl.ds(h, 1)
        log_ref[one, :] = -(step_ref[one, :] * rate_ref[h])

    cl_ref[...] = jnp.dot(log_ref[...], upper, precision=HI, preferred_element_type=F32)

    @pl.loop(0, XW // TILE)
    def _(i):
        cols = pl.ds(pl.multiple_of(i * TILE, TILE), TILE)
        dyt_ref[cols, :] = dy_ref[:, cols].astype(F32).T.astype(BF16)

    @pl.when(me == 0)
    def _():
        before_ref[...] = jnp.zeros_like(before_ref)

    @pl.when(me > 0)
    def _():
        rim_in.wait_recv()

    @pl.when(me < n - 1)
    def _():
        rim_in.wait_send()

    def send(src, dst, ss, rs, to):
        return pltpu.make_async_remote_copy(
            src_ref=src, dst_ref=dst, send_sem=ss, recv_sem=rs,
            device_id={"seq": to}, device_id_type=MESH,
        )

    def part(c):
        return pl.ds(c * CHUNK, CHUNK)

    def pair_copy(j, c):
        src, dst = ((s_ref, sp), (u_ref, up))[j]
        return send(
            src.at[pl.ds(other + c * CHUNK, CHUNK)], dst.at[part(c)],
            send1.at[j, c], recv1.at[j, c], pair,
        )

    def chain_copy(j, c):
        src, dst = ((eout, ein), (gout, gin))[j]
        return send(
            src.at[part(c)], dst.at[part(c)], send2.at[j, c], recv2.at[j, c],
            me + 2 if j == 0 else me - 2,
        )

    def back_copy(j, c):
        src, dst = ((sout, start_ref), (uout, end_ref))[j]
        return send(
            src.at[part(c)], dst.at[pl.ds(mine + c * CHUNK, CHUNK)],
            send3.at[j, c], recv3.at[j, c], pair,
        )

    decay_copy = send(dec_ref, ap, senda, recva, pair)

    def begin(j):
        @pl.loop(0, NCHUNK)
        def _(c):
            pair_copy(j, c).start()

    def run(j):
        has_in = z > 0 if j == 0 else z < last
        has_out = z < last if j == 0 else z > 0
        inbox, outbox = ((ein, eout), (gin, gout))[j]
        got, own, back, result = ((sp, s_ref, sout, start_ref), (up, u_ref, uout, end_ref))[j]

        @pl.when(jnp.logical_not(has_in))
        def _():
            inbox[...] = jnp.zeros_like(inbox)

        @pl.loop(0, NCHUNK)
        def _(c):
            pair_copy(j, c).wait_recv()
            here = pl.ds(mine + c * CHUNK, CHUNK)
            first = y == 0
            aa = dec_ref[here, :][:, None, :]
            bb = ap[here, :][:, None, :]
            a0 = jnp.where(first, aa, bb)
            a1 = jnp.where(first, bb, aa)
            vv = own[here].astype(F32)
            ww = got[part(c)].astype(F32)
            v0 = jnp.where(first, vv, ww)
            v1 = jnp.where(first, ww, vv)

            @pl.when(has_in)
            def _():
                chain_copy(j, c).wait_recv()

            carry = inbox[part(c)].astype(F32)
            if j == 0:
                near, far = carry, a0 * carry + v0
                leave = a1 * far + v1
                kept = jnp.where(first, near, far)
                given = jnp.where(first, far, near)
            else:
                far, near = carry, a1 * carry + v1
                leave = a0 * near + v0
                kept = jnp.where(first, near, far)
                given = jnp.where(first, far, near)
            outbox[part(c)] = leave.astype(BF16)

            @pl.when(has_out)
            def _():
                chain_copy(j, c).start()

            back[part(c)] = given.astype(BF16)
            back_copy(j, c).start()
            result[here] = kept.astype(BF16)

    def form(j):
        src, dst = ((xw_ref, s_ref), (dw_ref, u_ref))[j]
        cols = pl.ds(j * STATE, STATE)

        @pl.loop(0, XW // TILE)
        def _(i):
            rows = pl.ds(pl.multiple_of(i * TILE, TILE), TILE)
            value = dot(src[rows, :], bc_ref[:, cols], 1, 0).astype(BF16)
            dst[pl.ds(4 * i, 4)] = value.reshape(4, HEAD_DIM, STATE)

    def activate(cols):
        x = xbc_ref[:, cols].astype(F32)
        padded = jnp.concatenate([before_ref[:, cols].astype(F32), x], axis=0)
        pre = bias_ref[cols][None, :]
        for k in range(KCONV):
            pre = pre + w_ref[k : k + 1, cols] * padded[5 + k : 5 + k + GROUP]
        sig = 1.0 / (1.0 + jnp.exp(-pre))
        der_ref[:, cols] = sig * (1.0 + pre * (1.0 - sig))
        return pre * sig

    @pl.loop(0, XW // TILE)
    def _(i):
        cols = pl.ds(pl.multiple_of(i * TILE, TILE), TILE)
        zt_ref[cols, :] = activate(cols).T.astype(BF16)

    tail_z = activate(pl.ds(XW, TILE))
    bc_ref[...] = tail_z.astype(BF16)
    zt_ref[pl.ds(XW, TILE), :] = tail_z.T.astype(BF16)
    cum = cl_ref[...]
    dec_ref[...] = jnp.broadcast_to(jnp.exp(cum[:, GROUP - 1 : GROUP]), (HEADS, STATE))

    @pl.loop(0, HEADS)
    def _(h):
        rows = pl.ds(pl.multiple_of(h * HEAD_DIM, HEAD_DIM), HEAD_DIM)
        cl = cl_ref[pl.ds(h, 1), :]
        xw_ref[rows, :] = (
            zt_ref[rows, :].astype(F32) * jnp.exp(cl[:, GROUP - 1 : GROUP] - cl)
        ).astype(BF16)
        dw_ref[rows, :] = (dyt_ref[rows, :].astype(F32) * jnp.exp(cl)).astype(BF16)

    @pl.when(low)
    def _():
        form(0)
        begin(0)
        form(1)
        begin(1)

    @pl.when(jnp.logical_not(low))
    def _():
        form(1)
        begin(1)
        form(0)
        begin(0)

    decay_copy.start()
    bproj = bc_ref[:, :STATE]
    cproj = bc_ref[:, STATE:]
    gram_ref[...] = dot(cproj, bproj, 1, 1)
    wsum_ref[...] = jnp.zeros_like(wsum_ref)

    def inner_head(h):
        rows = pl.ds(pl.multiple_of(h * HEAD_DIM, HEAD_DIM), HEAD_DIM)
        xt = zt_ref[rows, :]
        dyt = dyt_ref[rows, :]
        cl = cl_ref[pl.ds(h, 1), :]
        wide = jnp.broadcast_to(cl, (STATE, GROUP)).T
        gap = jnp.concatenate([wide, wide], axis=1) - cl
        decay = jnp.where(causal, jnp.exp(gap), 0.0)
        kmat = (decay * gram_ref[...]).astype(BF16)
        intra = dot(dyt, kmat, 1, 0)
        yt = dot(xt, kmat, 1, 1)
        xf = xt.astype(F32)
        dyf = dyt.astype(F32)
        one = pl.ds(h, 1)
        intra_ref[rows, :] = intra
        d_ref[one, :] = jnp.sum(xf * intra - dyf * yt, axis=0, keepdims=True)
        k_ref[one, :] = jnp.sum(xf * dyf, axis=0, keepdims=True)
        return decay * dot(dyt, xt, 0, 0)

    def inner_heads(start):
        @pl.loop(0, HALF // 2)
        def _(i):
            h = start + 2 * i
            wsum_ref[...] += inner_head(h) + inner_head(h + 1)

    inner_heads(0)
    decay_copy.wait_recv()

    @pl.when(low)
    def _():
        run(0)

    @pl.when(jnp.logical_not(low))
    def _():
        run(1)

    inner_heads(HALF)

    @pl.when(low)
    def _():
        run(1)

    @pl.when(jnp.logical_not(low))
    def _():
        run(0)

    decay_copy.wait_send()
    for j in range(2):
        @pl.loop(0, NCHUNK)
        def _(c):
            pair_copy(j, c).wait_send()
            back_copy(j, c).wait()

            @pl.when(z < last if j == 0 else z > 0)
            def _():
                chain_copy(j, c).wait_send()


    def head(h):
        rows = pl.ds(pl.multiple_of(h * HEAD_DIM, HEAD_DIM), HEAD_DIM)
        cl = cl_ref[pl.ds(h, 1), :]
        adj = end_ref[h]
        sta = start_ref[h]
        badj = dot(adj, zt_ref[pl.ds(XW, STATE), :], 1, 0)
        cst = dot(sta, zt_ref[pl.ds(XW + STATE, STATE), :], 1, 0)
        log_end = cl[:, GROUP - 1 : GROUP]
        tail = jnp.exp(log_end - cl)
        xf = zt_ref[rows, :].astype(F32)
        dyf = dyt_ref[rows, :].astype(F32)
        rterm = tail * jnp.sum(xf * badj, axis=0, keepdims=True)
        qterm = jnp.exp(cl) * jnp.sum(dyf * cst, axis=0, keepdims=True)
        prod = adj.astype(F32) * sta.astype(F32)
        four = jnp.exp(log_end) * jnp.sum(jnp.sum(prod, axis=0, keepdims=True), axis=1, keepdims=True)
        one = pl.ds(h, 1)
        gain = d_ref[one, :] + rterm
        d_ref[one, :] = gain
        q_ref[one, :] = qterm
        l_ref[one, :] = four - gain
        return intra_ref[rows, :] + tail * badj + skip_ref[h] * dyf

    @pl.loop(0, HEADS // 2)
    def _(hp):
        both = jnp.concatenate([head(2 * hp), head(2 * hp + 1)], axis=0)
        gz_ref[:, pl.ds(pl.multiple_of(hp * STATE, STATE), STATE)] = both.T

    wlow = wsum_ref[...].astype(BF16)
    gb = dot(wlow, cproj, 0, 0) + dot(end_ref[...].reshape(XW, STATE), xw_ref[...], 0, 0).T
    gc = dot(wlow, bproj, 1, 0) + dot(start_ref[...].reshape(XW, STATE), dw_ref[...], 0, 0).T
    gz_ref[:, pl.ds(XW, STATE)] = gb
    gz_ref[:, pl.ds(XW + STATE, STATE)] = gc
    lower = (row >= col).astype(F32)
    glog = jnp.dot(d_ref[...], upper, precision=HI, preferred_element_type=F32)
    glog = glog + jnp.dot(q_ref[...], lower, precision=HI, preferred_element_type=F32)
    glog = glog + l_ref[...]
    d_ref[...] = glog

    @pl.loop(0, HEADS)
    def _(h):
        one = pl.ds(h, 1)
        gstep_ref[one, :] = -(d_ref[one, :] * rate_ref[h])

    ones = jnp.ones((8, GROUP), F32)
    sums = (-step_ref[...] * glog, k_ref[...])
    for c in range(2):
        line = lax.dot_general(
            ones, sums[c], (((1,), (1,)), ((), ())), precision=HI, preferred_element_type=F32
        )
        line = jnp.concatenate([line[:1], jnp.zeros((1, STATE - HEADS), F32)], axis=1)
        pack_ref[c, PACK - 1 : PACK, :] = line

    @pl.loop(0, CH // TILE)
    def _(i):
        cols = pl.ds(pl.multiple_of(i * TILE, TILE), TILE)
        gp = gz_ref[:, cols] * der_ref[:, cols]
        padded = jnp.concatenate([gp, jnp.zeros((8, TILE), F32)], axis=0)
        gin = w_ref[KCONV - 1 : KCONV, cols] * gp
        for k in range(KCONV - 1):
            off = KCONV - 1 - k
            gin = gin + w_ref[k : k + 1, cols] * padded[off : off + GROUP]
        gin_ref[:, cols] = gin.astype(BF16)
        edge_ref[:, cols] = gin[GROUP - EDGE :]
        first = gp[:8]
        sub = lax.broadcasted_iota(jnp.int32, (8, TILE), 0)
        front_pad = jnp.concatenate([jnp.zeros((8, TILE), F32), first], axis=0)
        rim = jnp.zeros((8, TILE), F32)
        for k in range(KCONV - 1):
            off = KCONV - 1 - k
            piece = jnp.where(sub >= 8 - off, front_pad[off : off + 8], 0.0)
            rim = rim + w_ref[k : k + 1, cols] * piece
        front_ref[:, cols] = rim
        x = jnp.concatenate([before_ref[:, cols].astype(F32), xbc_ref[:, cols].astype(F32)], axis=0)
        for k in range(KCONV + 1):
            terms = gp * x[5 + k : 5 + k + GROUP] if k < KCONV else gp
            line = jnp.sum(terms, axis=0, keepdims=True)
            for c in range(2):
                pack_ref[c, pl.ds(k * LINES + i, 1), :] = line[:, c * STATE : (c + 1) * STATE]

    rim = pltpu.make_async_remote_copy(
        src_ref=front_ref, dst_ref=rim_ref, send_sem=fs, recv_sem=fr,
        device_id={"seq": me - 1}, device_id_type=MESH,
    )

    @pl.when(me > 0)
    def _():
        rim.start()

    copies = []
    for i, where in enumerate(to):
        copy = pltpu.make_async_remote_copy(
            src_ref=pack_ref.at[1 - core] if i == 0 else acc.at[i], dst_ref=box.at[i],
            send_sem=ssem.at[i], recv_sem=rsem.at[i],
            device_id=where, device_id_type=MESH,
        )
        copy.start()
        copies.append(copy)
        copy.wait_recv()
        total = (pack_ref[core] if i == 0 else acc[i]) + box[i]
        acc[i + 1] = total
    share = pltpu.make_async_remote_copy(
        src_ref=acc.at[len(to)], dst_ref=out_ref.at[core], send_sem=gs, recv_sem=gr,
        device_id=to[0], device_id_type=MESH,
    )
    share.start()
    out_ref[core] = total
    share.wait()
    for copy in copies:
        copy.wait_send()

    @pl.when(me > 0)
    def _():
        rim.wait_send()

    @pl.when(me < n - 1)
    def _():
        rim.wait_recv()

    @pl.when(me == n - 1)
    def _():
        rim_ref[...] = jnp.zeros_like(rim_ref)


def finish_kernel(
    total_ref, edge_ref, rim_ref, gin_ref, out_ref, gw_ref, gb_ref, grate_ref, gskip_ref, last, sem
):
    final = edge_ref[...] + jnp.concatenate([jnp.zeros((8, CH), F32), rim_ref[...]], axis=0)
    last[...] = final.astype(BF16)
    copy = pltpu.make_async_copy(last, out_ref.at[pl.ds(GROUP - EDGE, EDGE)], sem)
    copy.start()
    for i in range(LINES):
        for c in range(2):
            cols = pl.ds((2 * i + c) * STATE, STATE)
            for k in range(KCONV):
                gw_ref[k : k + 1, cols] = total_ref[c, pl.ds(k * LINES + i, 1), :]
            gb_ref[cols] = total_ref[c, KCONV * LINES + i, :]
    grate_ref[...] = total_ref[0, PACK - 1, :HEADS]
    gskip_ref[...] = total_ref[1, PACK - 1, :HEADS]
    copy.wait()


def sds(shape, dtype):
    return jax.ShapeDtypeStruct(shape, dtype)


LIMIT = 62 * 1024 * 1024


def shards(xbc_in, conv_weight, conv_bias, step_sizes, decay_rates, skip_gain, grad_out):
    steps = [("dp", b) for b in bits_of(lax.axis_size("dp"))]
    steps += [("seq", b) for b in bits_of(lax.axis_size("seq"))]
    count = len(steps)
    state = (HEADS, HEAD_DIM, STATE)
    half = (HALF, HEAD_DIM, STATE)
    line = (HEADS, GROUP)
    dma = pltpu.SemaphoreType.DMA
    scratch = [
        ((CH, GROUP), BF16), ((GROUP, 2 * STATE), BF16), ((XW, GROUP), BF16), ((GROUP, CH), F32),
        (line, F32), ((XW, GROUP), BF16), ((XW, GROUP), BF16), (line, F32), ((8, CH), BF16),
        (state, BF16), (state, BF16), ((HEADS, STATE), F32), (state, BF16), (state, BF16),
        (half, BF16), (half, BF16), ((HEADS, STATE), F32),
    ]
    scratch += [(half, BF16)] * 6
    scratch += [((GROUP, GROUP), F32)] * 2 + [((XW, GROUP), F32), ((GROUP, CH), F32)]
    scratch += [(line, F32)] * 4 + [((8, CH), F32), ((2, PACK, STATE), F32)]
    scratch += [((count + 1, PACK, STATE), F32)] * 2
    gin, edge, gstep, total, rim = pl.pallas_call(
        functools.partial(core_kernel, steps),
        out_shape=[
            sds((GROUP, CH), BF16), sds((EDGE, CH), F32), sds((HEADS, GROUP), F32),
            sds((2, PACK, STATE), F32), sds((8, CH), F32),
        ],
        in_specs=[VM()] * 4 + [SM(), VM(), SM()],
        out_specs=[VM()] * 5,
        scratch_shapes=[pltpu.VMEM(*item) for item in scratch]
        + [dma((2, NCHUNK))] * 6
        + [dma] * 2
        + [dma((count,))] * 2
        + [dma] * 6,
        compiler_params=pltpu.CompilerParams(
            vmem_limit_bytes=LIMIT, collective_id=0, has_side_effects=True
        ),
    )(
        xbc_in[0], conv_weight, conv_bias, step_sizes[0], decay_rates, grad_out[0], skip_gain
    )
    grad_in, gw, gb, grate, gskip = pl.pallas_call(
        finish_kernel,
        out_shape=[
            sds((GROUP, CH), BF16), sds((KCONV, CH), F32), sds((CH,), F32),
            sds((HEADS,), F32), sds((HEADS,), F32),
        ],
        in_specs=[VM()] * 3 + [pl.BlockSpec(memory_space=pl.ANY)],
        out_specs=[pl.BlockSpec(memory_space=pl.ANY)] + [VM()] * 4,
        scratch_shapes=[pltpu.VMEM((EDGE, CH), BF16), dma],
        input_output_aliases={3: 0},
    )(total, edge, rim, gin)
    return (grad_in[None], gstep[None], gw, gb, grate, gskip)


def solution(mesh):
    return jax.shard_map(
        shards,
        mesh=mesh,
        in_specs=(
            P("dp", "seq", None), P(), P(), P("dp", None, "seq"), P(), P(), P("dp", "seq", None),
        ),
        out_specs=(P("dp", "seq", None), P("dp", None, "seq"), P(), P(), P(), P()),
        check_vma=False,
    )
```

```python
import functools
import jax
import jax.numpy as jnp
from jax import lax
from jax.experimental import pallas as pl
from jax.experimental.pallas import tpu as pltpu
from jax.sharding import PartitionSpec as P

HEADS = 40
HEAD_DIM = 64
STATE = 128
GROUP = 256
KCONV = 4
XW = HEADS * HEAD_DIM
CH = XW + 2 * STATE
TILE = 256
HALF = HEADS // 2
CHUNK = 2
EDGE = 16
LINES = CH // TILE
PACK = (KCONV + 1) * LINES + 1
NCHUNK = HALF // CHUNK
MESH = pl.DeviceIdType.MESH
F32 = jnp.float32
BF16 = jnp.bfloat16
HI = lax.Precision.HIGHEST
VM = functools.partial(pl.BlockSpec, memory_space=pltpu.VMEM)
SM = functools.partial(pl.BlockSpec, memory_space=pltpu.SMEM)


def dot(a, b, ca, cb):
    return lax.dot_general(a, b, (((ca,), (cb,)), ((), ())), preferred_element_type=F32)


def bits_of(n):
    out = []
    b = 1
    while b < n:
        out.append(b)
        b *= 2
    return out


def core_kernel(
    steps,
    xbc_ref, w_ref, bias_ref, step_ref, rate_ref, dy_ref, skip_ref,
    gin_ref, edge_ref, gstep_ref, out_ref, rim_ref,
    zt_ref, bc_ref, dyt_ref, der_ref, cl_ref, xw_ref, dw_ref, log_ref, before_ref,
    s_ref, u_ref, dec_ref, start_ref, end_ref,
    sp, up, ap, ein, gin, eout, gout, sout, uout,
    gram_ref, wsum_ref, intra_ref, gz_ref, d_ref, q_ref, l_ref, k_ref, front_ref, pack_ref,
    acc, box,
    send1, recv1, send2, recv2, send3, recv3, senda, recva,
    ssem, rsem, fs, fr, gs, gr, bs, br,
):
    pos = {"dp": lax.axis_index("dp"), "seq": lax.axis_index("seq")}
    me = pos["seq"]
    n = lax.axis_size("seq")
    core = pos["dp"] % 2
    y = me % 2
    z = me // 2
    nz = n // 2
    pair = me + 1 - 2 * y
    mine = y * HALF
    other = (1 - y) * HALF
    last = nz - 1
    low = z < nz - nz // 2
    to = []
    for axis, b in steps:
        p = pos[axis]
        to.append({axis: p + b * (1 - 2 * ((p // b) % 2))})
    barrier = pltpu.get_barrier_semaphore()
    for where in to + [{"seq": pair}]:
        pl.semaphore_signal(barrier, inc=1, device_id=where, device_id_type=MESH)
    edges = 0
    for by in (-2, -1, 1, 2):
        inside = me + by >= 0 if by < 0 else me + by < n
        edges = edges + jnp.where(inside, 1, 0)

        @pl.when(inside)
        def _():
            pl.semaphore_signal(barrier, inc=1, device_id={"seq": me + by}, device_id_type=MESH)

    pl.semaphore_wait(barrier, len(to) + 1 + edges)

    rim_in = pltpu.make_async_remote_copy(
        src_ref=xbc_ref.at[pl.ds(GROUP - 8, 8)], dst_ref=before_ref, send_sem=bs, recv_sem=br,
        device_id={"seq": me + 1}, device_id_type=MESH,
    )

    @pl.when(me < n - 1)
    def _():
        rim_in.start()

    row = lax.broadcasted_iota(jnp.int32, (GROUP, GROUP), 0)
    col = lax.broadcasted_iota(jnp.int32, (GROUP, GROUP), 1)
    causal = row >= col
    upper = (row <= col).astype(F32)

    @pl.loop(0, HEADS)
    def _(h):
        one = pl.ds(h, 1)
        log_ref[one, :] = -(step_ref[one, :] * rate_ref[h])

    cl_ref[...] = jnp.dot(log_ref[...], upper, precision=HI, preferred_element_type=F32)

    @pl.loop(0, XW // TILE)
    def _(i):
        cols = pl.ds(pl.multiple_of(i * TILE, TILE), TILE)
        dyt_ref[cols, :] = dy_ref[:, cols].astype(F32).T.astype(BF16)

    @pl.when(me == 0)
    def _():
        before_ref[...] = jnp.zeros_like(before_ref)

    @pl.when(me > 0)
    def _():
        rim_in.wait_recv()

    @pl.when(me < n - 1)
    def _():
        rim_in.wait_send()

    def send(src, dst, ss, rs, to):
        return pltpu.make_async_remote_copy(
            src_ref=src, dst_ref=dst, send_sem=ss, recv_sem=rs,
            device_id={"seq": to}, device_id_type=MESH,
        )

    def part(c):
        return pl.ds(c * CHUNK, CHUNK)

    def pair_copy(j, c):
        src, dst = ((s_ref, sp), (u_ref, up))[j]
        return send(
            src.at[pl.ds(other + c * CHUNK, CHUNK)], dst.at[part(c)],
            send1.at[j, c], recv1.at[j, c], pair,
        )

    def chain_copy(j, c):
        src, dst = ((eout, ein), (gout, gin))[j]
        return send(
            src.at[part(c)], dst.at[part(c)], send2.at[j, c], recv2.at[j, c],
            me + 2 if j == 0 else me - 2,
        )

    def back_copy(j, c):
        src, dst = ((sout, start_ref), (uout, end_ref))[j]
        return send(
            src.at[part(c)], dst.at[pl.ds(mine + c * CHUNK, CHUNK)],
            send3.at[j, c], recv3.at[j, c], pair,
        )

    decay_copy = send(dec_ref, ap, senda, recva, pair)

    def begin(j):
        @pl.loop(0, NCHUNK)
        def _(c):
            pair_copy(j, c).start()

    def run(j):
        has_in = z > 0 if j == 0 else z < last
        has_out = z < last if j == 0 else z > 0
        inbox, outbox = ((ein, eout), (gin, gout))[j]
        got, own, back, result = ((sp, s_ref, sout, start_ref), (up, u_ref, uout, end_ref))[j]

        @pl.when(jnp.logical_not(has_in))
        def _():
            inbox[...] = jnp.zeros_like(inbox)

        @pl.loop(0, NCHUNK)
        def _(c):
            pair_copy(j, c).wait_recv()
            here = pl.ds(mine + c * CHUNK, CHUNK)
            first = y == 0
            aa = dec_ref[here, :][:, None, :]
            bb = ap[here, :][:, None, :]
            a0 = jnp.where(first, aa, bb)
            a1 = jnp.where(first, bb, aa)
            vv = own[here].astype(F32)
            ww = got[part(c)].astype(F32)
            v0 = jnp.where(first, vv, ww)
            v1 = jnp.where(first, ww, vv)

            @pl.when(has_in)
            def _():
                chain_copy(j, c).wait_recv()

            carry = inbox[part(c)].astype(F32)
            if j == 0:
                near, far = carry, a0 * carry + v0
                leave = a1 * far + v1
                kept = jnp.where(first, near, far)
                given = jnp.where(first, far, near)
            else:
                far, near = carry, a1 * carry + v1
                leave = a0 * near + v0
                kept = jnp.where(first, near, far)
                given = jnp.where(first, far, near)
            outbox[part(c)] = leave.astype(BF16)

            @pl.when(has_out)
            def _():
                chain_copy(j, c).start()

            back[part(c)] = given.astype(BF16)
            back_copy(j, c).start()
            result[here] = kept.astype(BF16)

    def form(j):
        src, dst = ((xw_ref, s_ref), (dw_ref, u_ref))[j]
        cols = pl.ds(j * STATE, STATE)

        @pl.loop(0, XW // TILE)
        def _(i):
            rows = pl.ds(pl.multiple_of(i * TILE, TILE), TILE)
            value = dot(src[rows, :], bc_ref[:, cols], 1, 0).astype(BF16)
            dst[pl.ds(4 * i, 4)] = value.reshape(4, HEAD_DIM, STATE)

    def activate(cols):
        x = xbc_ref[:, cols].astype(F32)
        padded = jnp.concatenate([before_ref[:, cols].astype(F32), x], axis=0)
        pre = bias_ref[cols][None, :]
        for k in range(KCONV):
            pre = pre + w_ref[k : k + 1, cols] * padded[5 + k : 5 + k + GROUP]
        sig = 1.0 / (1.0 + jnp.exp(-pre))
        der_ref[:, cols] = sig * (1.0 + pre * (1.0 - sig))
        return pre * sig

    tail_z = activate(pl.ds(XW, TILE))
    bc_ref[...] = tail_z.astype(BF16)
    zt_ref[pl.ds(XW, TILE), :] = tail_z.T.astype(BF16)
    cum = cl_ref[...]
    dec_ref[...] = jnp.broadcast_to(jnp.exp(cum[:, GROUP - 1 : GROUP]), (HEADS, STATE))

    @pl.loop(0, HEADS)
    def _(h):
        rows = pl.ds(pl.multiple_of(h * HEAD_DIM, HEAD_DIM), HEAD_DIM)
        cl = cl_ref[pl.ds(h, 1), :]
        dw_ref[rows, :] = (dyt_ref[rows, :].astype(F32) * jnp.exp(cl)).astype(BF16)

    form(1)
    begin(1)

    @pl.loop(0, XW // TILE)
    def _(i):
        cols = pl.ds(pl.multiple_of(i * TILE, TILE), TILE)
        zt_ref[cols, :] = activate(cols).T.astype(BF16)

    @pl.loop(0, HEADS)
    def _(h):
        rows = pl.ds(pl.multiple_of(h * HEAD_DIM, HEAD_DIM), HEAD_DIM)
        cl = cl_ref[pl.ds(h, 1), :]
        xw_ref[rows, :] = (
            zt_ref[rows, :].astype(F32) * jnp.exp(cl[:, GROUP - 1 : GROUP] - cl)
        ).astype(BF16)

    form(0)
    begin(0)

    decay_copy.start()
    bproj = bc_ref[:, :STATE]
    cproj = bc_ref[:, STATE:]
    gram_ref[...] = dot(cproj, bproj, 1, 1)
    wsum_ref[...] = jnp.zeros_like(wsum_ref)

    def inner_head(h):
        rows = pl.ds(pl.multiple_of(h * HEAD_DIM, HEAD_DIM), HEAD_DIM)
        xt = zt_ref[rows, :]
        dyt = dyt_ref[rows, :]
        cl = cl_ref[pl.ds(h, 1), :]
        wide = jnp.broadcast_to(cl, (STATE, GROUP)).T
        gap = jnp.concatenate([wide, wide], axis=1) - cl
        decay = jnp.where(causal, jnp.exp(gap), 0.0)
        kmat = (decay * gram_ref[...]).astype(BF16)
        intra = dot(dyt, kmat, 1, 0)
        yt = dot(xt, kmat, 1, 1)
        xf = xt.astype(F32)
        dyf = dyt.astype(F32)
        one = pl.ds(h, 1)
        intra_ref[rows, :] = intra
        d_ref[one, :] = jnp.sum(xf * intra - dyf * yt, axis=0, keepdims=True)
        k_ref[one, :] = jnp.sum(xf * dyf, axis=0, keepdims=True)
        return decay * dot(dyt, xt, 0, 0)

    def inner_heads(start):
        @pl.loop(0, HALF // 2)
        def _(i):
            h = start + 2 * i
            wsum_ref[...] += inner_head(h) + inner_head(h + 1)

    inner_heads(0)
    decay_copy.wait_recv()

    @pl.when(low)
    def _():
        run(0)

    @pl.when(jnp.logical_not(low))
    def _():
        run(1)

    inner_heads(HALF)

    @pl.when(low)
    def _():
        run(1)

    @pl.when(jnp.logical_not(low))
    def _():
        run(0)

    decay_copy.wait_send()
    for j in range(2):
        @pl.loop(0, NCHUNK)
        def _(c):
            pair_copy(j, c).wait_send()
            back_copy(j, c).wait()

            @pl.when(z < last if j == 0 else z > 0)
            def _():
                chain_copy(j, c).wait_send()


    def head(h):
        rows = pl.ds(pl.multiple_of(h * HEAD_DIM, HEAD_DIM), HEAD_DIM)
        cl = cl_ref[pl.ds(h, 1), :]
        adj = end_ref[h]
        sta = start_ref[h]
        badj = dot(adj, zt_ref[pl.ds(XW, STATE), :], 1, 0)
        cst = dot(sta, zt_ref[pl.ds(XW + STATE, STATE), :], 1, 0)
        log_end = cl[:, GROUP - 1 : GROUP]
        tail = jnp.exp(log_end - cl)
        xf = zt_ref[rows, :].astype(F32)
        dyf = dyt_ref[rows, :].astype(F32)
        rterm = tail * jnp.sum(xf * badj, axis=0, keepdims=True)
        qterm = jnp.exp(cl) * jnp.sum(dyf * cst, axis=0, keepdims=True)
        prod = adj.astype(F32) * sta.astype(F32)
        four = jnp.exp(log_end) * jnp.sum(jnp.sum(prod, axis=0, keepdims=True), axis=1, keepdims=True)
        one = pl.ds(h, 1)
        gain = d_ref[one, :] + rterm
        d_ref[one, :] = gain
        q_ref[one, :] = qterm
        l_ref[one, :] = four - gain
        return intra_ref[rows, :] + tail * badj + skip_ref[h] * dyf

    @pl.loop(0, HEADS // 2)
    def _(hp):
        both = jnp.concatenate([head(2 * hp), head(2 * hp + 1)], axis=0)
        gz_ref[:, pl.ds(pl.multiple_of(hp * STATE, STATE), STATE)] = both.T

    wlow = wsum_ref[...].astype(BF16)
    gb = dot(wlow, cproj, 0, 0) + dot(end_ref[...].reshape(XW, STATE), xw_ref[...], 0, 0).T
    gc = dot(wlow, bproj, 1, 0) + dot(start_ref[...].reshape(XW, STATE), dw_ref[...], 0, 0).T
    gz_ref[:, pl.ds(XW, STATE)] = gb
    gz_ref[:, pl.ds(XW + STATE, STATE)] = gc
    lower = (row >= col).astype(F32)
    glog = jnp.dot(d_ref[...], upper, precision=HI, preferred_element_type=F32)
    glog = glog + jnp.dot(q_ref[...], lower, precision=HI, preferred_element_type=F32)
    glog = glog + l_ref[...]
    d_ref[...] = glog

    @pl.loop(0, HEADS)
    def _(h):
        one = pl.ds(h, 1)
        gstep_ref[one, :] = -(d_ref[one, :] * rate_ref[h])

    ones = jnp.ones((8, GROUP), F32)
    sums = (-step_ref[...] * glog, k_ref[...])
    for c in range(2):
        line = lax.dot_general(
            ones, sums[c], (((1,), (1,)), ((), ())), precision=HI, preferred_element_type=F32
        )
        line = jnp.concatenate([line[:1], jnp.zeros((1, STATE - HEADS), F32)], axis=1)
        pack_ref[c, PACK - 1 : PACK, :] = line

    @pl.loop(0, CH // TILE)
    def _(i):
        cols = pl.ds(pl.multiple_of(i * TILE, TILE), TILE)
        gp = gz_ref[:, cols] * der_ref[:, cols]
        padded = jnp.concatenate([gp, jnp.zeros((8, TILE), F32)], axis=0)
        gin = w_ref[KCONV - 1 : KCONV, cols] * gp
        for k in range(KCONV - 1):
            off = KCONV - 1 - k
            gin = gin + w_ref[k : k + 1, cols] * padded[off : off + GROUP]
        gin_ref[:, cols] = gin.astype(BF16)
        edge_ref[:, cols] = gin[GROUP - EDGE :]
        first = gp[:8]
        sub = lax.broadcasted_iota(jnp.int32, (8, TILE), 0)
        front_pad = jnp.concatenate([jnp.zeros((8, TILE), F32), first], axis=0)
        rim = jnp.zeros((8, TILE), F32)
        for k in range(KCONV - 1):
            off = KCONV - 1 - k
            piece = jnp.where(sub >= 8 - off, front_pad[off : off + 8], 0.0)
            rim = rim + w_ref[k : k + 1, cols] * piece
        front_ref[:, cols] = rim
        x = jnp.concatenate([before_ref[:, cols].astype(F32), xbc_ref[:, cols].astype(F32)], axis=0)
        for k in range(KCONV + 1):
            terms = gp * x[5 + k : 5 + k + GROUP] if k < KCONV else gp
            line = jnp.sum(terms, axis=0, keepdims=True)
            for c in range(2):
                pack_ref[c, pl.ds(k * LINES + i, 1), :] = line[:, c * STATE : (c + 1) * STATE]

    rim = pltpu.make_async_remote_copy(
        src_ref=front_ref, dst_ref=rim_ref, send_sem=fs, recv_sem=fr,
        device_id={"seq": me - 1}, device_id_type=MESH,
    )

    @pl.when(me > 0)
    def _():
        rim.start()

    copies = []
    for i, where in enumerate(to):
        copy = pltpu.make_async_remote_copy(
            src_ref=pack_ref.at[1 - core] if i == 0 else acc.at[i], dst_ref=box.at[i],
            send_sem=ssem.at[i], recv_sem=rsem.at[i],
            device_id=where, device_id_type=MESH,
        )
        copy.start()
        copies.append(copy)
        copy.wait_recv()
        total = (pack_ref[core] if i == 0 else acc[i]) + box[i]
        acc[i + 1] = total
    share = pltpu.make_async_remote_copy(
        src_ref=acc.at[len(to)], dst_ref=out_ref.at[core], send_sem=gs, recv_sem=gr,
        device_id=to[0], device_id_type=MESH,
    )
    share.start()
    out_ref[core] = total
    share.wait()
    for copy in copies:
        copy.wait_send()

    @pl.when(me > 0)
    def _():
        rim.wait_send()

    @pl.when(me < n - 1)
    def _():
        rim.wait_recv()

    @pl.when(me == n - 1)
    def _():
        rim_ref[...] = jnp.zeros_like(rim_ref)


def finish_kernel(
    total_ref, edge_ref, rim_ref, gin_ref, out_ref, gw_ref, gb_ref, grate_ref, gskip_ref, last, sem
):
    final = edge_ref[...] + jnp.concatenate([jnp.zeros((8, CH), F32), rim_ref[...]], axis=0)
    last[...] = final.astype(BF16)
    copy = pltpu.make_async_copy(last, out_ref.at[pl.ds(GROUP - EDGE, EDGE)], sem)
    copy.start()
    for i in range(LINES):
        for c in range(2):
            cols = pl.ds((2 * i + c) * STATE, STATE)
            for k in range(KCONV):
                gw_ref[k : k + 1, cols] = total_ref[c, pl.ds(k * LINES + i, 1), :]
            gb_ref[cols] = total_ref[c, KCONV * LINES + i, :]
    grate_ref[...] = total_ref[0, PACK - 1, :HEADS]
    gskip_ref[...] = total_ref[1, PACK - 1, :HEADS]
    copy.wait()


def sds(shape, dtype):
    return jax.ShapeDtypeStruct(shape, dtype)


LIMIT = 62 * 1024 * 1024


def shards(xbc_in, conv_weight, conv_bias, step_sizes, decay_rates, skip_gain, grad_out):
    steps = [("dp", b) for b in bits_of(lax.axis_size("dp"))]
    steps += [("seq", b) for b in bits_of(lax.axis_size("seq"))]
    count = len(steps)
    state = (HEADS, HEAD_DIM, STATE)
    half = (HALF, HEAD_DIM, STATE)
    line = (HEADS, GROUP)
    dma = pltpu.SemaphoreType.DMA
    scratch = [
        ((CH, GROUP), BF16), ((GROUP, 2 * STATE), BF16), ((XW, GROUP), BF16), ((GROUP, CH), F32),
        (line, F32), ((XW, GROUP), BF16), ((XW, GROUP), BF16), (line, F32), ((8, CH), BF16),
        (state, BF16), (state, BF16), ((HEADS, STATE), F32), (state, BF16), (state, BF16),
        (half, BF16), (half, BF16), ((HEADS, STATE), F32),
    ]
    scratch += [(half, BF16)] * 6
    scratch += [((GROUP, GROUP), F32)] * 2 + [((XW, GROUP), F32), ((GROUP, CH), F32)]
    scratch += [(line, F32)] * 4 + [((8, CH), F32), ((2, PACK, STATE), F32)]
    scratch += [((count + 1, PACK, STATE), F32)] * 2
    gin, edge, gstep, total, rim = pl.pallas_call(
        functools.partial(core_kernel, steps),
        out_shape=[
            sds((GROUP, CH), BF16), sds((EDGE, CH), F32), sds((HEADS, GROUP), F32),
            sds((2, PACK, STATE), F32), sds((8, CH), F32),
        ],
        in_specs=[VM()] * 4 + [SM(), VM(), SM()],
        out_specs=[VM()] * 5,
        scratch_shapes=[pltpu.VMEM(*item) for item in scratch]
        + [dma((2, NCHUNK))] * 6
        + [dma] * 2
        + [dma((count,))] * 2
        + [dma] * 6,
        compiler_params=pltpu.CompilerParams(
            vmem_limit_bytes=LIMIT, collective_id=0, has_side_effects=True
        ),
    )(
        xbc_in[0], conv_weight, conv_bias, step_sizes[0], decay_rates, grad_out[0], skip_gain
    )
    grad_in, gw, gb, grate, gskip = pl.pallas_call(
        finish_kernel,
        out_shape=[
            sds((GROUP, CH), BF16), sds((KCONV, CH), F32), sds((CH,), F32),
            sds((HEADS,), F32), sds((HEADS,), F32),
        ],
        in_specs=[VM()] * 3 + [pl.BlockSpec(memory_space=pl.ANY)],
        out_specs=[pl.BlockSpec(memory_space=pl.ANY)] + [VM()] * 4,
        scratch_shapes=[pltpu.VMEM((EDGE, CH), BF16), dma],
        input_output_aliases={3: 0},
    )(total, edge, rim, gin)
    return (grad_in[None], gstep[None], gw, gb, grate, gskip)


def solution(mesh):
    return jax.shard_map(
        shards,
        mesh=mesh,
        in_specs=(
            P("dp", "seq", None), P(), P(), P("dp", None, "seq"), P(), P(), P("dp", "seq", None),
        ),
        out_specs=(P("dp", "seq", None), P("dp", None, "seq"), P(), P(), P(), P()),
        check_vma=False,
    )
```

```python
import functools
import jax
import jax.numpy as jnp
from jax import lax
from jax.experimental import pallas as pl
from jax.experimental.pallas import tpu as pltpu
from jax.sharding import PartitionSpec as P

HEADS = 40
HEAD_DIM = 64
STATE = 128
GROUP = 256
KCONV = 4
XW = HEADS * HEAD_DIM
CH = XW + 2 * STATE
TILE = 256
HALF = HEADS // 2
CHUNK = 2
EDGE = 16
LINES = CH // TILE
PACK = (KCONV + 1) * LINES + 1
NCHUNK = HALF // CHUNK
MESH = pl.DeviceIdType.MESH
F32 = jnp.float32
BF16 = jnp.bfloat16
HI = lax.Precision.HIGHEST
VM = functools.partial(pl.BlockSpec, memory_space=pltpu.VMEM)
SM = functools.partial(pl.BlockSpec, memory_space=pltpu.SMEM)


def dot(a, b, ca, cb):
    return lax.dot_general(a, b, (((ca,), (cb,)), ((), ())), preferred_element_type=F32)


def bits_of(n):
    out = []
    b = 1
    while b < n:
        out.append(b)
        b *= 2
    return out


def core_kernel(
    steps,
    xbc_ref, w_ref, bias_ref, step_ref, rate_ref, dy_ref, skip_ref,
    gin_ref, edge_ref, gstep_ref, out_ref, rim_ref,
    zt_ref, bc_ref, dyt_ref, der_ref, cl_ref, xw_ref, dw_ref, log_ref, before_ref,
    s_ref, u_ref, dec_ref, start_ref, end_ref,
    sp, up, ap, ein, gin, eout, gout, sout, uout,
    gram_ref, wsum_ref, intra_ref, gz_ref, d_ref, q_ref, l_ref, k_ref, front_ref, pack_ref,
    acc, box,
    send1, recv1, send2, recv2, send3, recv3, senda, recva,
    ssem, rsem, fs, fr, gs, gr, bs, br,
):
    pos = {"dp": lax.axis_index("dp"), "seq": lax.axis_index("seq")}
    me = pos["seq"]
    n = lax.axis_size("seq")
    core = pos["dp"] % 2
    y = me % 2
    z = me // 2
    nz = n // 2
    pair = me + 1 - 2 * y
    mine = y * HALF
    other = (1 - y) * HALF
    last = nz - 1
    low = z < nz - nz // 2
    to = []
    for axis, b in steps:
        p = pos[axis]
        to.append({axis: p + b * (1 - 2 * ((p // b) % 2))})
    barrier = pltpu.get_barrier_semaphore()
    for where in to + [{"seq": pair}]:
        pl.semaphore_signal(barrier, inc=1, device_id=where, device_id_type=MESH)
    edges = 0
    for by in (-2, -1, 1, 2):
        inside = me + by >= 0 if by < 0 else me + by < n
        edges = edges + jnp.where(inside, 1, 0)

        @pl.when(inside)
        def _():
            pl.semaphore_signal(barrier, inc=1, device_id={"seq": me + by}, device_id_type=MESH)

    pl.semaphore_wait(barrier, len(to) + 1 + edges)

    rim_in = pltpu.make_async_remote_copy(
        src_ref=xbc_ref.at[pl.ds(GROUP - 8, 8)], dst_ref=before_ref, send_sem=bs, recv_sem=br,
        device_id={"seq": me + 1}, device_id_type=MESH,
    )

    @pl.when(me < n - 1)
    def _():
        rim_in.start()

    row = lax.broadcasted_iota(jnp.int32, (GROUP, GROUP), 0)
    col = lax.broadcasted_iota(jnp.int32, (GROUP, GROUP), 1)
    causal = row >= col
    upper = (row <= col).astype(F32)

    @pl.loop(0, HEADS)
    def _(h):
        one = pl.ds(h, 1)
        log_ref[one, :] = -(step_ref[one, :] * rate_ref[h])

    cl_ref[...] = jnp.dot(log_ref[...], upper, precision=HI, preferred_element_type=F32)

    @pl.loop(0, XW // TILE)
    def _(i):
        cols = pl.ds(pl.multiple_of(i * TILE, TILE), TILE)
        dyt_ref[cols, :] = dy_ref[:, cols].astype(F32).T.astype(BF16)

    @pl.when(me == 0)
    def _():
        before_ref[...] = jnp.zeros_like(before_ref)

    @pl.when(me > 0)
    def _():
        rim_in.wait_recv()

    @pl.when(me < n - 1)
    def _():
        rim_in.wait_send()

    def send(src, dst, ss, rs, to):
        return pltpu.make_async_remote_copy(
            src_ref=src, dst_ref=dst, send_sem=ss, recv_sem=rs,
            device_id={"seq": to}, device_id_type=MESH,
        )

    def part(c):
        return pl.ds(c * CHUNK, CHUNK)

    def pair_copy(j, c):
        src, dst = ((s_ref, sp), (u_ref, up))[j]
        return send(
            src.at[pl.ds(other + c * CHUNK, CHUNK)], dst.at[part(c)],
            send1.at[j, c], recv1.at[j, c], pair,
        )

    def chain_copy(j, c):
        src, dst = ((eout, ein), (gout, gin))[j]
        return send(
            src.at[part(c)], dst.at[part(c)], send2.at[j, c], recv2.at[j, c],
            me + 2 if j == 0 else me - 2,
        )

    def back_copy(j, c):
        src, dst = ((sout, start_ref), (uout, end_ref))[j]
        return send(
            src.at[part(c)], dst.at[pl.ds(mine + c * CHUNK, CHUNK)],
            send3.at[j, c], recv3.at[j, c], pair,
        )

    decay_copy = send(dec_ref, ap, senda, recva, pair)

    def begin(j):
        @pl.loop(0, NCHUNK)
        def _(c):
            pair_copy(j, c).start()

    def run(j):
        has_in = z > 0 if j == 0 else z < last
        has_out = z < last if j == 0 else z > 0
        inbox, outbox = ((ein, eout), (gin, gout))[j]
        got, own, back, result = ((sp, s_ref, sout, start_ref), (up, u_ref, uout, end_ref))[j]

        @pl.when(jnp.logical_not(has_in))
        def _():
            inbox[...] = jnp.zeros_like(inbox)

        @pl.loop(0, NCHUNK)
        def _(c):
            pair_copy(j, c).wait_recv()
            here = pl.ds(mine + c * CHUNK, CHUNK)
            first = y == 0
            aa = dec_ref[here, :][:, None, :]
            bb = ap[here, :][:, None, :]
            a0 = jnp.where(first, aa, bb)
            a1 = jnp.where(first, bb, aa)
            vv = own[here].astype(F32)
            ww = got[part(c)].astype(F32)
            v0 = jnp.where(first, vv, ww)
            v1 = jnp.where(first, ww, vv)

            @pl.when(has_in)
            def _():
                chain_copy(j, c).wait_recv()

            carry = inbox[part(c)].astype(F32)
            if j == 0:
                near, far = carry, a0 * carry + v0
                leave = a1 * far + v1
                kept = jnp.where(first, near, far)
                given = jnp.where(first, far, near)
            else:
                far, near = carry, a1 * carry + v1
                leave = a0 * near + v0
                kept = jnp.where(first, near, far)
                given = jnp.where(first, far, near)
            outbox[part(c)] = leave.astype(BF16)

            @pl.when(has_out)
            def _():
                chain_copy(j, c).start()

            back[part(c)] = given.astype(BF16)
            back_copy(j, c).start()
            result[here] = kept.astype(BF16)

    def form(j):
        src, dst = ((xw_ref, s_ref), (dw_ref, u_ref))[j]
        cols = pl.ds(j * STATE, STATE)

        @pl.loop(0, XW // TILE)
        def _(i):
            rows = pl.ds(pl.multiple_of(i * TILE, TILE), TILE)
            value = dot(src[rows, :], bc_ref[:, cols], 1, 0).astype(BF16)
            dst[pl.ds(4 * i, 4)] = value.reshape(4, HEAD_DIM, STATE)

    def activate(cols):
        x = xbc_ref[:, cols].astype(F32)
        padded = jnp.concatenate([before_ref[:, cols].astype(F32), x], axis=0)
        pre = bias_ref[cols][None, :]
        for k in range(KCONV):
            pre = pre + w_ref[k : k + 1, cols] * padded[5 + k : 5 + k + GROUP]
        sig = 1.0 / (1.0 + jnp.exp(-pre))
        der_ref[:, cols] = sig * (1.0 + pre * (1.0 - sig))
        return pre * sig

    tail_z = activate(pl.ds(XW, TILE))
    bc_ref[...] = tail_z.astype(BF16)
    zt_ref[pl.ds(XW, TILE), :] = tail_z.T.astype(BF16)
    cum = cl_ref[...]
    dec_ref[...] = jnp.broadcast_to(jnp.exp(cum[:, GROUP - 1 : GROUP]), (HEADS, STATE))

    @pl.loop(0, HEADS)
    def _(h):
        rows = pl.ds(pl.multiple_of(h * HEAD_DIM, HEAD_DIM), HEAD_DIM)
        cl = cl_ref[pl.ds(h, 1), :]
        dw_ref[rows, :] = (dyt_ref[rows, :].astype(F32) * jnp.exp(cl)).astype(BF16)

    form(1)
    begin(1)

    @pl.loop(0, XW // TILE)
    def _(i):
        cols = pl.ds(pl.multiple_of(i * TILE, TILE), TILE)
        zt_ref[cols, :] = activate(cols).T.astype(BF16)

    @pl.loop(0, HEADS)
    def _(h):
        rows = pl.ds(pl.multiple_of(h * HEAD_DIM, HEAD_DIM), HEAD_DIM)
        cl = cl_ref[pl.ds(h, 1), :]
        xw_ref[rows, :] = (
            zt_ref[rows, :].astype(F32) * jnp.exp(cl[:, GROUP - 1 : GROUP] - cl)
        ).astype(BF16)

    form(0)
    begin(0)

    decay_copy.start()
    bproj = bc_ref[:, :STATE]
    cproj = bc_ref[:, STATE:]
    gram_ref[...] = dot(cproj, bproj, 1, 1)
    wsum_ref[...] = jnp.zeros_like(wsum_ref)

    def inner_head(h):
        rows = pl.ds(pl.multiple_of(h * HEAD_DIM, HEAD_DIM), HEAD_DIM)
        xt = zt_ref[rows, :]
        dyt = dyt_ref[rows, :]
        cl = cl_ref[pl.ds(h, 1), :]
        wide = jnp.broadcast_to(cl, (STATE, GROUP)).T
        gap = jnp.concatenate([wide, wide], axis=1) - cl
        decay = jnp.where(causal, jnp.exp(gap), 0.0)
        kmat = (decay * gram_ref[...]).astype(BF16)
        intra = dot(dyt, kmat, 1, 0)
        yt = dot(xt, kmat, 1, 1)
        xf = xt.astype(F32)
        dyf = dyt.astype(F32)
        one = pl.ds(h, 1)
        intra_ref[rows, :] = intra
        d_ref[one, :] = jnp.sum(xf * intra - dyf * yt, axis=0, keepdims=True)
        k_ref[one, :] = jnp.sum(xf * dyf, axis=0, keepdims=True)
        return decay * dot(dyt, xt, 0, 0)

    def inner_heads(start):
        @pl.loop(0, HALF // 4)
        def _(i):
            h = start + 4 * i
            front = inner_head(h) + inner_head(h + 1)
            wsum_ref[...] += front + (inner_head(h + 2) + inner_head(h + 3))

    inner_heads(0)
    decay_copy.wait_recv()

    @pl.when(low)
    def _():
        run(0)

    @pl.when(jnp.logical_not(low))
    def _():
        run(1)

    inner_heads(HALF)

    @pl.when(low)
    def _():
        run(1)

    @pl.when(jnp.logical_not(low))
    def _():
        run(0)

    decay_copy.wait_send()
    for j in range(2):
        @pl.loop(0, NCHUNK)
        def _(c):
            pair_copy(j, c).wait_send()
            back_copy(j, c).wait()

            @pl.when(z < last if j == 0 else z > 0)
            def _():
                chain_copy(j, c).wait_send()


    def head(h):
        rows = pl.ds(pl.multiple_of(h * HEAD_DIM, HEAD_DIM), HEAD_DIM)
        cl = cl_ref[pl.ds(h, 1), :]
        adj = end_ref[h]
        sta = start_ref[h]
        badj = dot(adj, zt_ref[pl.ds(XW, STATE), :], 1, 0)
        cst = dot(sta, zt_ref[pl.ds(XW + STATE, STATE), :], 1, 0)
        log_end = cl[:, GROUP - 1 : GROUP]
        tail = jnp.exp(log_end - cl)
        xf = zt_ref[rows, :].astype(F32)
        dyf = dyt_ref[rows, :].astype(F32)
        rterm = tail * jnp.sum(xf * badj, axis=0, keepdims=True)
        qterm = jnp.exp(cl) * jnp.sum(dyf * cst, axis=0, keepdims=True)
        prod = adj.astype(F32) * sta.astype(F32)
        four = jnp.exp(log_end) * jnp.sum(jnp.sum(prod, axis=0, keepdims=True), axis=1, keepdims=True)
        one = pl.ds(h, 1)
        gain = d_ref[one, :] + rterm
        d_ref[one, :] = gain
        q_ref[one, :] = qterm
        l_ref[one, :] = four - gain
        return intra_ref[rows, :] + tail * badj + skip_ref[h] * dyf

    @pl.loop(0, HEADS // 4)
    def _(hp):
        four = jnp.concatenate([head(4 * hp + j) for j in range(4)], axis=0)
        gz_ref[:, pl.ds(pl.multiple_of(hp * TILE, TILE), TILE)] = four.T

    wlow = wsum_ref[...].astype(BF16)
    gb = dot(wlow, cproj, 0, 0) + dot(end_ref[...].reshape(XW, STATE), xw_ref[...], 0, 0).T
    gc = dot(wlow, bproj, 1, 0) + dot(start_ref[...].reshape(XW, STATE), dw_ref[...], 0, 0).T
    gz_ref[:, pl.ds(XW, STATE)] = gb
    gz_ref[:, pl.ds(XW + STATE, STATE)] = gc
    lower = (row >= col).astype(F32)
    glog = jnp.dot(d_ref[...], upper, precision=HI, preferred_element_type=F32)
    glog = glog + jnp.dot(q_ref[...], lower, precision=HI, preferred_element_type=F32)
    glog = glog + l_ref[...]
    d_ref[...] = glog

    @pl.loop(0, HEADS)
    def _(h):
        one = pl.ds(h, 1)
        gstep_ref[one, :] = -(d_ref[one, :] * rate_ref[h])

    ones = jnp.ones((8, GROUP), F32)
    sums = (-step_ref[...] * glog, k_ref[...])
    for c in range(2):
        line = lax.dot_general(
            ones, sums[c], (((1,), (1,)), ((), ())), precision=HI, preferred_element_type=F32
        )
        line = jnp.concatenate([line[:1], jnp.zeros((1, STATE - HEADS), F32)], axis=1)
        pack_ref[c, PACK - 1 : PACK, :] = line

    @pl.loop(0, CH // TILE)
    def _(i):
        cols = pl.ds(pl.multiple_of(i * TILE, TILE), TILE)
        gp = gz_ref[:, cols] * der_ref[:, cols]
        padded = jnp.concatenate([gp, jnp.zeros((8, TILE), F32)], axis=0)
        gin = w_ref[KCONV - 1 : KCONV, cols] * gp
        for k in range(KCONV - 1):
            off = KCONV - 1 - k
            gin = gin + w_ref[k : k + 1, cols] * padded[off : off + GROUP]
        gin_ref[:, cols] = gin.astype(BF16)
        edge_ref[:, cols] = gin[GROUP - EDGE :]
        first = gp[:8]
        sub = lax.broadcasted_iota(jnp.int32, (8, TILE), 0)
        front_pad = jnp.concatenate([jnp.zeros((8, TILE), F32), first], axis=0)
        rim = jnp.zeros((8, TILE), F32)
        for k in range(KCONV - 1):
            off = KCONV - 1 - k
            piece = jnp.where(sub >= 8 - off, front_pad[off : off + 8], 0.0)
            rim = rim + w_ref[k : k + 1, cols] * piece
        front_ref[:, cols] = rim
        x = jnp.concatenate([before_ref[:, cols].astype(F32), xbc_ref[:, cols].astype(F32)], axis=0)
        for k in range(KCONV + 1):
            terms = gp * x[5 + k : 5 + k + GROUP] if k < KCONV else gp
            line = jnp.sum(terms, axis=0, keepdims=True)
            for c in range(2):
                pack_ref[c, pl.ds(k * LINES + i, 1), :] = line[:, c * STATE : (c + 1) * STATE]

    rim = pltpu.make_async_remote_copy(
        src_ref=front_ref, dst_ref=rim_ref, send_sem=fs, recv_sem=fr,
        device_id={"seq": me - 1}, device_id_type=MESH,
    )

    @pl.when(me > 0)
    def _():
        rim.start()

    copies = []
    for i, where in enumerate(to):
        copy = pltpu.make_async_remote_copy(
            src_ref=pack_ref.at[1 - core] if i == 0 else acc.at[i], dst_ref=box.at[i],
            send_sem=ssem.at[i], recv_sem=rsem.at[i],
            device_id=where, device_id_type=MESH,
        )
        copy.start()
        copies.append(copy)
        copy.wait_recv()
        total = (pack_ref[core] if i == 0 else acc[i]) + box[i]
        acc[i + 1] = total
    share = pltpu.make_async_remote_copy(
        src_ref=acc.at[len(to)], dst_ref=out_ref.at[core], send_sem=gs, recv_sem=gr,
        device_id=to[0], device_id_type=MESH,
    )
    share.start()
    out_ref[core] = total
    share.wait()
    for copy in copies:
        copy.wait_send()

    @pl.when(me > 0)
    def _():
        rim.wait_send()

    @pl.when(me < n - 1)
    def _():
        rim.wait_recv()

    @pl.when(me == n - 1)
    def _():
        rim_ref[...] = jnp.zeros_like(rim_ref)


def finish_kernel(
    total_ref, edge_ref, rim_ref, gin_ref, out_ref, gw_ref, gb_ref, grate_ref, gskip_ref, last, sem
):
    final = edge_ref[...] + jnp.concatenate([jnp.zeros((8, CH), F32), rim_ref[...]], axis=0)
    last[...] = final.astype(BF16)
    copy = pltpu.make_async_copy(last, out_ref.at[pl.ds(GROUP - EDGE, EDGE)], sem)
    copy.start()
    for i in range(LINES):
        for c in range(2):
            cols = pl.ds((2 * i + c) * STATE, STATE)
            for k in range(KCONV):
                gw_ref[k : k + 1, cols] = total_ref[c, pl.ds(k * LINES + i, 1), :]
            gb_ref[cols] = total_ref[c, KCONV * LINES + i, :]
    grate_ref[...] = total_ref[0, PACK - 1, :HEADS]
    gskip_ref[...] = total_ref[1, PACK - 1, :HEADS]
    copy.wait()


def sds(shape, dtype):
    return jax.ShapeDtypeStruct(shape, dtype)


LIMIT = 62 * 1024 * 1024


def shards(xbc_in, conv_weight, conv_bias, step_sizes, decay_rates, skip_gain, grad_out):
    steps = [("dp", b) for b in bits_of(lax.axis_size("dp"))]
    steps += [("seq", b) for b in bits_of(lax.axis_size("seq"))]
    count = len(steps)
    state = (HEADS, HEAD_DIM, STATE)
    half = (HALF, HEAD_DIM, STATE)
    line = (HEADS, GROUP)
    dma = pltpu.SemaphoreType.DMA
    scratch = [
        ((CH, GROUP), BF16), ((GROUP, 2 * STATE), BF16), ((XW, GROUP), BF16), ((GROUP, CH), F32),
        (line, F32), ((XW, GROUP), BF16), ((XW, GROUP), BF16), (line, F32), ((8, CH), BF16),
        (state, BF16), (state, BF16), ((HEADS, STATE), F32), (state, BF16), (state, BF16),
        (half, BF16), (half, BF16), ((HEADS, STATE), F32),
    ]
    scratch += [(half, BF16)] * 6
    scratch += [((GROUP, GROUP), F32)] * 2 + [((XW, GROUP), F32), ((GROUP, CH), F32)]
    scratch += [(line, F32)] * 4 + [((8, CH), F32), ((2, PACK, STATE), F32)]
    scratch += [((count + 1, PACK, STATE), F32)] * 2
    gin, edge, gstep, total, rim = pl.pallas_call(
        functools.partial(core_kernel, steps),
        out_shape=[
            sds((GROUP, CH), BF16), sds((EDGE, CH), F32), sds((HEADS, GROUP), F32),
            sds((2, PACK, STATE), F32), sds((8, CH), F32),
        ],
        in_specs=[VM()] * 4 + [SM(), VM(), SM()],
        out_specs=[VM()] * 5,
        scratch_shapes=[pltpu.VMEM(*item) for item in scratch]
        + [dma((2, NCHUNK))] * 6
        + [dma] * 2
        + [dma((count,))] * 2
        + [dma] * 6,
        compiler_params=pltpu.CompilerParams(
            vmem_limit_bytes=LIMIT, collective_id=0, has_side_effects=True
        ),
    )(
        xbc_in[0], conv_weight, conv_bias, step_sizes[0], decay_rates, grad_out[0], skip_gain
    )
    grad_in, gw, gb, grate, gskip = pl.pallas_call(
        finish_kernel,
        out_shape=[
            sds((GROUP, CH), BF16), sds((KCONV, CH), F32), sds((CH,), F32),
            sds((HEADS,), F32), sds((HEADS,), F32),
        ],
        in_specs=[VM()] * 3 + [pl.BlockSpec(memory_space=pl.ANY)],
        out_specs=[pl.BlockSpec(memory_space=pl.ANY)] + [VM()] * 4,
        scratch_shapes=[pltpu.VMEM((EDGE, CH), BF16), dma],
        input_output_aliases={3: 0},
    )(total, edge, rim, gin)
    return (grad_in[None], gstep[None], gw, gb, grate, gskip)


def solution(mesh):
    return jax.shard_map(
        shards,
        mesh=mesh,
        in_specs=(
            P("dp", "seq", None), P(), P(), P("dp", None, "seq"), P(), P(), P("dp", "seq", None),
        ),
        out_specs=(P("dp", "seq", None), P("dp", None, "seq"), P(), P(), P(), P()),
        check_vma=False,
    )
```
